32 devices in a mesh: layer: 4 (over y, core), feat: 4 (over z), path: 2 (over x).
Axes of the slice: x: 2, y: 2, z: 4, core: 2. Of those that a mesh axis runs over, the one named last changes fastest.
Arguments:
- context: bfloat16 [4, 64, 2304], P('layer'), may hold values from -6 to 6
- targets: bfloat16 [4, 64, 2304], P('layer'), may hold values from -4 to 4
- beyond_targets: bfloat16 [64, 2304], replicated, may hold values from -4 to 4
- positions: int32 [32], replicated, may hold values from 0 to 63
- donors: int32 [32], replicated, may hold values from 0 to 63
- encoder: bfloat16 [4, 2304, 8192], P('layer', None, 'feat'), may hold values from -0.125 to 0.125
- encoder_bias: float32 [4, 8192], P('layer', 'feat'), may hold values from -3 to 3
- decoder: bfloat16 [4, 2, 8192, 2304], P('layer', None, 'feat', 'path'), may hold values from -0.0625 to 0.0625
Outputs:
- attribution: float32 [4, 32, 2304], P('layer', None, ('feat', 'path'))
The draws below stay inside these ranges and needn't reach their ends.
All inputs are finite; a program needn't handle non-finite values.
Results may differ from the reference program's by a relative error of at most 0.0071.
Values may be sent and summed in bfloat16 or wider, within the bound.
A program may use at most 64 MiB of HBM per device.

```python
import jax
import jax.numpy as jnp

D = 2304
F = 8192
LAYERS = 4
ROWS_PT = 32
CTX = 64
PTS_DEV = 4
N_PATH = 2


def with_ends(drawn, key, least, top_value):
    longest = drawn.shape.index(max(drawn.shape))
    spots = []
    for shift in (0, 1):
        where = [jax.random.randint(jax.random.fold_in(key, axis), (), 0, length) for axis, length in enumerate(drawn.shape)]
        where[longest] = (where[longest] + shift) % drawn.shape[longest]
        spots.append(tuple(where))
    return drawn.at[spots[0]].set(least).at[spots[1]].set(top_value)


def levels(rng, extent, cuts, smallest, largest):
    loudness = 1.0
    for dim, blocks in cuts:
        draws = jax.random.uniform(jax.random.fold_in(jax.random.fold_in(rng, 6), dim), (blocks,), jnp.float32, smallest / len(cuts), largest / len(cuts))
        loudness = loudness * jnp.repeat(jnp.exp(draws), extent[dim] // blocks).reshape((-1,) + (1,) * (len(extent) - 1 - dim))
    return loudness


def noise(own_key, extent, spread, limit, split=(), kind=jnp.bfloat16):
    drawn = spread * jax.random.normal(own_key, extent, jnp.float32)
    if split:
        drawn = drawn * levels(own_key, extent, split, -0.22, 0.18)
    return jnp.clip(drawn, -limit, limit).astype(kind)


def setup_inputs(seed: int = 0) -> dict:
    streams_of = jax.random.split(jax.random.key(seed), 9)
    context = noise(streams_of[0], (LAYERS, CTX, D), 1.0, 6.0, ((0, 4),))
    targets = noise(streams_of[1], (LAYERS, CTX, D), 0.5, 4.0, ((0, 4),))
    beyond_targets = noise(streams_of[2], (CTX, D), 0.5, 4.0)
    positions = with_ends(jax.random.randint(streams_of[3], (ROWS_PT,), 0, CTX), jax.random.fold_in(streams_of[3], 1), 0, CTX - 1).astype(jnp.int32)
    donors = with_ends(jax.random.randint(streams_of[4], (ROWS_PT,), 0, CTX), jax.random.fold_in(streams_of[4], 1), 0, CTX - 1).astype(jnp.int32)
    encoder = noise(streams_of[5], (LAYERS, D, F), D ** -0.5, 0.125, ((0, 4), (2, 4)))
    encoder_bias = noise(streams_of[6], (LAYERS, F), 0.5, 3.0, ((0, 4), (1, 4)), jnp.float32)
    decoder = noise(streams_of[7], (LAYERS, 2, F, D), F ** -0.5, 0.0625, ((0, 4), (2, 4), (3, 2)))
    return {"context": context, "targets": targets, "beyond_targets": beyond_targets, "positions": positions, "donors": donors, "encoder": encoder, "encoder_bias": encoder_bias, "decoder": decoder}


def reference(context, targets, beyond_targets, positions, donors, encoder, encoder_bias, decoder):
    points = PTS_DEV * N_PATH
    fraction = (jnp.arange(points).astype(jnp.float32) + 0.5) / points
    offsets = []
    preacts = []
    parts = []
    for source in range(LAYERS):
        source_rows = context[source][positions].astype(jnp.float32)
        donor_rows = context[source][donors].astype(jnp.float32)
        offset = source_rows - donor_rows
        inputs = (donor_rows[None] + fraction[:, None, None] * offset[None]).astype(jnp.bfloat16).reshape(-1, D)
        preact = jnp.dot(inputs, encoder[source], preferred_element_type=jnp.float32) + encoder_bias[source]
        code_rows = jnp.maximum(preact, 0.0).astype(jnp.bfloat16)
        here = jnp.dot(code_rows, decoder[source, 0], preferred_element_type=jnp.float32)
        later = jnp.dot(code_rows, decoder[source, 1], preferred_element_type=jnp.float32)
        offsets.append(offset)
        preacts.append(preact)
        parts.append((here, later))
    errors = []
    for target in range(LAYERS + 1):
        if target == LAYERS:
            rebuilt = parts[LAYERS - 1][1]
            goal_rows = beyond_targets[positions].astype(jnp.float32)
        else:
            rebuilt = parts[target][0]
            if target > 0:
                rebuilt = rebuilt + parts[target - 1][1]
            goal_rows = targets[target][positions].astype(jnp.float32)
        rebuilt = rebuilt.reshape(points, ROWS_PT, D)
        errors.append((rebuilt - goal_rows[None]).astype(jnp.bfloat16).reshape(-1, D))
    results = []
    for source in range(LAYERS):
        grads = jnp.dot(errors[source], decoder[source, 0].T, preferred_element_type=jnp.float32)
        grads = grads + jnp.dot(errors[source + 1], decoder[source, 1].T, preferred_element_type=jnp.float32)
        gated = jnp.where(preacts[source] > 0, grads, 0.0).astype(jnp.bfloat16)
        input_grads = jnp.dot(gated, encoder[source].T, preferred_element_type=jnp.float32)
        summed = input_grads.reshape(points, ROWS_PT, D).sum(axis=0)
        results.append(offsets[source] * summed / points)
    return jnp.stack(results)
```

```python
import functools

import jax
import jax.numpy as jnp
from jax import lax
from jax.experimental import pallas as pl
from jax.experimental.pallas import tpu as pltpu
from jax.sharding import PartitionSpec as P

PTS_DEV = 4
EARLY = 2
MEET_LAG = 3
HOP_LAG = 9
SIDE_LAG = 3
SLACK = 1
MESH = pl.DeviceIdType.MESH
NT = (((1,), (1,)), ((), ()))
F32, BF16 = jnp.float32, jnp.bfloat16


def tile_of(width, most):
    sizes = [t for t in range(128, most + 1, 128) if width % t == 0]
    return sizes[-1] if sizes else width


def aligned(start, size):
    return pl.ds(pl.multiple_of(start, size), size)


def chunk_of(cols):
    return 128 if cols % 128 == 0 else cols


def decode_tiles(ncol):
    tiles, at = [], 0
    while at < ncol:
        take = min(2 if at == 0 else 4, ncol - at)
        if ncol - at - take == 1:
            take = min(3, ncol - at)
        if ncol - at == 3:
            take = 3
        tiles.append((at, take))
        at += take
    return tiles


def kernel(
    shape, pos_ref, don_ref, bias_ref, ctx_hbm, tgt_hbm, bey_hbm, enc_hbm, dec_hbm, out_ref,
    enc, dec, ctx, table, inputs, codes, own, away, away_in, goal, send, recv, err, gsum, part, offsets, final_send, final_recv,
    enc_sem, dec_sem, load_sem, part_sem, in_send, in_recv, err_sem, back_sem, final_sem,
):
    layers, n, paths = shape
    layer, z, path = lax.axis_index("layer"), lax.axis_index("feat"), lax.axis_index("path")
    last = layers - 1
    height, tokens = pos_ref.shape[1], ctx.shape[0]
    rows, width = inputs.shape
    feats, cols = codes.shape[1], dec.shape[2]
    points = rows // height
    half = rows // 2
    cw = chunk_of(cols)
    ncol = cols // cw
    tiles = decode_tiles(ncol)
    groups = n * paths
    me = z * paths + path
    scatter = final_send is not None

    first = lax.rem(layer, 2)
    at_end = (layer == 0) | (layer == last)
    free = jnp.where(layer == 0, 0, 1)

    def has_neighbour(k):
        return jnp.where(k == 0, layer > 0, layer < last)

    def neighbour(k):
        return lax.rem(layer + 2 * k - 1 + layers, layers)

    low = n // 2
    upward = z < low
    depth = jnp.where(upward, z, n - 1 - z)
    to_meet = jnp.where(upward, low, n - low) - 1 - depth
    outermost, meets = depth == 0, to_meet == 0
    inner = lax.rem(jnp.where(upward, z + 1, z - 1 + n), n)
    outer = lax.rem(jnp.where(upward, z - 1 + n, z + 1), n)

    barrier = pltpu.get_barrier_semaphore()

    def greet(i, carry):
        pl.semaphore_signal(barrier, inc=1, device_id={"path": lax.rem(path + 1 + i, paths)}, device_id_type=MESH)
        return carry

    lax.fori_loop(0, paths - 1, greet, 0)

    @pl.when(z > 0)
    def _():
        pl.semaphore_signal(barrier, inc=1, device_id={"feat": z - 1}, device_id_type=MESH)

    @pl.when(z < n - 1)
    def _():
        pl.semaphore_signal(barrier, inc=1, device_id={"feat": z + 1}, device_id_type=MESH)

    @pl.when(layer > 0)
    def _():
        pl.semaphore_signal(barrier, inc=1, device_id={"layer": layer - 1}, device_id_type=MESH)

    @pl.when(layer < last)
    def _():
        pl.semaphore_signal(barrier, inc=1, device_id={"layer": layer + 1}, device_id_type=MESH)

    etile = tile_of(feats, 512)
    etiles = feats // etile
    ftile = tile_of(feats, 1024)
    ftiles = feats // ftile

    def enc_copy(j):
        return pltpu.make_async_copy(
            enc_hbm.at[0, :, aligned(j * etile, etile)], enc.at[:, aligned(j * etile, etile)], enc_sem.at[j]
        )

    def columns(at, take):
        return slice(None) if ncol == 1 else pl.ds(pl.multiple_of(at * cw, cw), take * cw)

    def dec_copy(k, i):
        at = columns(*tiles[i])
        return pltpu.make_async_copy(dec_hbm.at[0, k, :, at], dec.at[k, :, at], dec_sem.at[k, i])

    ctx_copy = pltpu.make_async_copy(ctx_hbm.at[0], ctx, load_sem.at[0])
    goal_at = slice(None) if tgt_hbm.shape[2] == cols else aligned(path * cols, cols)
    goal_copies = [
        pltpu.make_async_copy(tgt_hbm.at[0, :, goal_at], table.at[0], load_sem.at[1]),
        pltpu.make_async_copy(bey_hbm.at[:, goal_at], table.at[1], load_sem.at[2]),
    ]

    ctx_copy.start()
    for j in range(etiles):
        enc_copy(j).start()
    for copy in goal_copies:
        copy.start()

    token = lax.broadcasted_iota(jnp.int32, (tokens, height), 0)
    pick_source = (token == pos_ref[...]).astype(F32).T.astype(BF16)
    pick_donor = (token == don_ref[...]).astype(F32).T.astype(BF16)

    def pick(which, rows_of):
        return jnp.dot(which, rows_of, preferred_element_type=F32)

    ctx_copy.wait()
    donor = pick(pick_donor, ctx[...])
    offset = pick(pick_source, ctx[...]) - donor
    for p in range(points):
        inputs[p * height : (p + 1) * height, :] = (donor + ((p + 0.5) / points) * offset).astype(BF16)

    def encode(j, carry):
        enc_copy(j).wait()

        @pl.when(j == max(etiles - 2, 0))
        def _():
            for i in range(len(tiles)):
                for k in (first, 1 - first):
                    dec_copy(k, i).start()

        at = aligned(j * etile, etile)
        preact = jnp.dot(inputs[...], enc[:, at], preferred_element_type=F32) + bias_ref[:, at]
        codes[:, at] = jnp.maximum(preact, 0.0).astype(BF16)
        return carry

    lax.fori_loop(0, etiles, encode, 0)

    for copy in goal_copies:
        copy.wait()
    for k in (0, 1):
        value = pick(pick_source, table[k])
        value = jnp.where((z == low - 1) & ((k == 0) | (layer == last)), value, 0.0)
        for m in range(ncol):
            goal[k, m] = value[:, m * cw : (m + 1) * cw]

    around = jnp.minimum(z, 1) + jnp.minimum(n - 1 - z, 1) + jnp.minimum(layer, 1) + jnp.minimum(last - layer, 1)
    pl.semaphore_wait(barrier, paths - 1 + around)

    def half_rows(h):
        return aligned(h * half, half)

    def part_copy(k, i):
        at = pl.ds(*tiles[i])
        return pltpu.make_async_remote_copy(
            away.at[k, at], away_in.at[1 - k, at], part_sem.at[0, k, i], part_sem.at[1, 1 - k, i],
            device_id={"layer": neighbour(k)}, device_id_type=MESH,
        )

    def part_arrival(k, i):
        at = pl.ds(*tiles[i])
        return pltpu.make_async_remote_copy(
            away.at[k, at], away_in.at[k, at], part_sem.at[0, k, i], part_sem.at[1, k, i],
            device_id={"layer": neighbour(k)}, device_id_type=MESH,
        )

    def decode(k, i):
        dec_copy(k, i).wait()
        start, take = tiles[i]
        value = jnp.dot(codes[...], dec[k, :, columns(start, take)], preferred_element_type=F32)
        for c in range(take):
            here = value[:, c * cw : (c + 1) * cw].reshape(points, height, cw) - goal[k, start + c][None]
            own[k, start + c] = here.reshape(rows, cw)

        @pl.when(has_neighbour(k))
        def _():
            for c in range(take):
                away[k, start + c] = own[k, start + c, half_rows(k)].astype(BF16)
            part_copy(k, i).start()

    def in_copy(k, h, m):
        at = (m, half_rows(h))
        kind = jnp.where(meets, 1, 0)
        return pltpu.make_async_remote_copy(
            send.at[k, *at], recv.at[kind, k, *at], in_send.at[k, h, m], in_recv.at[kind, k, h, m],
            device_id={"feat": inner}, device_id_type=MESH,
        )

    def in_arrival(kind, k, h, m):
        at = (m, half_rows(h))
        return pltpu.make_async_remote_copy(
            send.at[k, *at], recv.at[kind, k, *at], in_send.at[k, h, m], in_recv.at[kind, k, h, m],
            device_id={"feat": inner}, device_id_type=MESH,
        )

    def err_copy(k, h, m):
        at = (m, half_rows(h))
        return pltpu.make_async_remote_copy(
            err.at[k, *at], err.at[k, *at], err_sem.at[0, k, h, m], err_sem.at[1, k, h, m],
            device_id={"feat": outer}, device_id_type=MESH,
        )

    def back_copy(k, m):
        at = (m, half_rows(1 - k))
        return pltpu.make_async_remote_copy(
            err.at[k, *at], err.at[1 - k, *at], back_sem.at[0, k, m], back_sem.at[1, 1 - k, m],
            device_id={"layer": neighbour(k)}, device_id_type=MESH,
        )

    def back_arrival(k, m):
        at = (m, half_rows(k))
        return pltpu.make_async_remote_copy(
            err.at[1 - k, *at], err.at[k, *at], back_sem.at[0, k, m], back_sem.at[1, k, m],
            device_id={"layer": neighbour(k)}, device_id_type=MESH,
        )

    def piece(p):
        k = jnp.where(p == 0, first, jnp.where(p == 1, free, 1 - first))
        h = jnp.where(p == 1, k, 1 - k)
        return k, h, (p != 1) | at_end, jnp.where((p == 2) & at_end, SIDE_LAG, 0)

    def inward(p, m):
        k, h, _, _ = piece(p)
        at = (m, half_rows(h))
        with_neighbour = has_neighbour(k)

        for i, (start, take) in enumerate(tiles):

            @pl.when(with_neighbour & (m == start))
            def _():
                part_arrival(k, i).wait_recv()

        @pl.when(with_neighbour)
        def _():
            own[k, *at] = own[k, *at] + away_in[k, m].astype(F32)

        @pl.when(outermost)
        def _():
            send[k, *at] = own[k, *at].astype(BF16)

        @pl.when(~outermost)
        def _():
            in_arrival(0, k, h, m).wait_recv()
            send[k, *at] = (own[k, *at] + recv[0, k, *at].astype(F32)).astype(BF16)

        in_copy(k, h, m).start()

    def finish(p, m):
        k, h, _, _ = piece(p)
        at = (m, half_rows(h))

        @pl.when(meets)
        def _():
            in_arrival(1, k, h, m).wait_recv()
            err[k, *at] = (send[k, *at].astype(F32) + recv[1, k, *at].astype(F32)).astype(BF16)

        @pl.when(~meets)
        def _():
            err_copy(k, h, m).wait_recv()

        @pl.when(~outermost)
        def _():
            err_copy(k, h, m).start()

        @pl.when(has_neighbour(k))
        def _():
            back_copy(k, m).start()

    def each_piece(act):
        def of(p, carry):
            act(p)
            return carry

        lax.fori_loop(0, 3, of, 0)

    pushed = at_end & outermost & (free == first)
    lag = MEET_LAG + HOP_LAG * to_meet
    behind = lag + SIDE_LAG + SLACK
    pairs = ncol // 2

    def grads_step(k, at, take):
        for c in range(take):

            @pl.when(has_neighbour(k))
            def _():
                back_arrival(k, at + c).wait_recv()

        here = columns(at, take)

        def of_tile(j, carry):
            f_at = aligned(j * ftile, ftile)
            errors = jnp.concatenate([err[k, at + c] for c in range(take)], axis=1)
            grads = lax.dot_general(errors, dec[k, f_at, here], NT, preferred_element_type=F32)
            gated = jnp.where(codes[:, f_at].astype(F32) > 0, grads, 0.0)
            gsum[:, f_at] += gated.reshape(points, height, ftile).sum(axis=0)
            return carry

        lax.fori_loop(0, ftiles, of_tile, 0)

    def both(act):
        def of(s, carry):
            act(jnp.where(s == 0, first, 1 - first))
            return carry

        lax.fori_loop(0, 2, of, 0)

    def step(m, carry):
        def of_piece(p):
            k, h, active, late = piece(p)
            i = m - late

            @pl.when(active & (i >= 0) & (i < ncol) & ~(pushed & (p != 2)))
            def _():
                inward(p, i)

            f = i - lag

            @pl.when(active & (f >= 0) & (f < ncol))
            def _():
                finish(p, f)

        each_piece(of_piece)
        return carry

    def step_and_grads(m, carry):
        step(m, carry)
        g = m - behind
        if pairs:

            @pl.when((g >= 1) & (g < 2 * pairs) & (lax.rem(g + 2, 2) == 1))
            def _():
                both(lambda k: grads_step(k, g - 1, 2))

        return carry

    gsum[...] = jnp.zeros_like(gsum)

    def push(i):
        @pl.when(pushed)
        def _():
            def of_column(m, carry):
                inward(0, m)
                inward(1, m)
                return carry

            lax.fori_loop(tiles[i][0], tiles[i][0] + tiles[i][1], of_column, 0)

    for i in range(len(tiles)):
        decode(first, i)
        push(i)
        decode(1 - first, i)
        if i == min(1, len(tiles) - 1):
            early = min(EARLY, ncol)

            @pl.when(at_end)
            def _():
                lax.fori_loop(0, early, step, 0)

    if scatter:
        block = width // groups
        for b in range(groups):
            offsets[b] = offset[:, b * block : (b + 1) * block]

    lax.fori_loop(jnp.where(at_end, early, 0), ncol + behind, step_and_grads, 0)
    if ncol % 2:
        both(lambda k: grads_step(k, ncol - 1, 1))

    if scatter:
        gated_sum = gsum[...].astype(BF16)

        def final_copy(sender, target):
            return pltpu.make_async_remote_copy(
                final_send.at[target], final_recv.at[sender], final_sem.at[0, target], final_sem.at[1, sender],
                device_id={"feat": target // paths, "path": lax.rem(target, paths)}, device_id_type=MESH,
            )

        side = groups // 2

        def send_side(i, carry):
            which = jnp.where(2 * z < n, 1 - i, i)
            at = aligned(which * side * block, side * block)
            product = lax.dot_general(gated_sum, enc[at, :], NT, preferred_element_type=F32)
            for c in range(side):
                b = which * side + c
                value = product[:, c * block : (c + 1) * block]

                @pl.when(b == me)
                def _():
                    part[...] = value

                @pl.when(b != me)
                def _():
                    final_send[b] = value.astype(BF16)
                    final_copy(me, b).start()

            return carry

        lax.fori_loop(0, 2, send_side, 0)

        def take_block(i, carry):
            b = lax.rem(me + 1 + i, groups)
            final_copy(b, b).wait_recv()
            part[...] += final_recv[b].astype(F32)
            return carry

        lax.fori_loop(0, groups - 1, take_block, 0)
        out_ref[...] = offsets[me] * part[...] / points

        def sent_block(i, carry):
            b = lax.rem(me + 1 + i, groups)
            final_copy(me, b).wait_send()
            return carry

        lax.fori_loop(0, groups - 1, sent_block, 0)
    else:
        out_ref[...] = lax.dot_general(gsum[...].astype(BF16), enc[...], NT, preferred_element_type=F32)

    for i in range(len(tiles)):
        for k in (0, 1):

            @pl.when(has_neighbour(k))
            def _():
                part_copy(k, i).wait_send()

    def sent(m, carry):
        def of_piece(p):
            k, h, active, _ = piece(p)

            @pl.when(active)
            def _():
                in_copy(k, h, m).wait_send()

                @pl.when(~outermost)
                def _():
                    err_copy(k, h, m).wait_send()

                @pl.when(has_neighbour(k))
                def _():
                    back_copy(k, m).wait_send()

        each_piece(of_piece)
        return carry

    lax.fori_loop(0, ncol, sent, 0)


def per_device(shape, context, targets, beyond_targets, positions, donors, encoder, encoder_bias, decoder):
    layers, n, paths = shape
    path = lax.axis_index("path")
    height = positions.shape[0]
    tokens = context.shape[1]
    width, feats = encoder.shape[1:]
    cols = decoder.shape[3]
    points = PTS_DEV * paths
    rows = points * height
    half = rows // 2
    groups = n * paths
    block = width // groups
    me = lax.axis_index("feat") * paths + path
    scatter = block % 16 == 0 and groups % 2 == 0
    if cols % 128:
        targets = lax.dynamic_slice_in_dim(targets, path * cols, cols, 2)
        beyond_targets = lax.dynamic_slice_in_dim(beyond_targets, path * cols, cols, 1)
    dma = pltpu.SemaphoreType.DMA
    cw = chunk_of(cols)
    ncol = cols // cw
    tiles = len(decode_tiles(ncol))
    final = (
        [
            pltpu.VMEM((height, block), F32),
            pltpu.VMEM((groups, height, block), F32),
            pltpu.VMEM((groups, height, block), BF16),
            pltpu.VMEM((groups, height, block), BF16),
        ]
        if scatter
        else [None, None, None, None]
    )
    scratch = [
        pltpu.VMEM((width, feats), BF16),
        pltpu.VMEM((2, feats, cols), BF16),
        pltpu.VMEM((tokens, width), BF16),
        pltpu.VMEM((2, tokens, cols), BF16),
        pltpu.VMEM((rows, width), BF16),
        pltpu.VMEM((rows, feats), BF16),
        pltpu.VMEM((2, ncol, rows, cw), F32),
        pltpu.VMEM((2, ncol, half, cw), BF16),
        pltpu.VMEM((2, ncol, half, cw), BF16),
        pltpu.VMEM((2, ncol, height, cw), F32),
        pltpu.VMEM((2, ncol, rows, cw), BF16),
        pltpu.VMEM((2, 2, ncol, rows, cw), BF16),
        pltpu.VMEM((2, ncol, rows, cw), BF16),
        pltpu.VMEM((height, feats), F32),
        *final,
        dma((feats // tile_of(feats, 512),)),
        dma((2, tiles)),
        dma((3,)),
        dma((2, 2, tiles)),
        dma((2, 2, ncol)),
        dma((2, 2, 2, ncol)),
        dma((2, 2, 2, ncol)),
        dma((2, 2, ncol)),
        dma((2, groups)) if scatter else None,
    ]
    kept = [s is not None for s in scratch]

    def body(*refs):
        fixed, given = refs[:9], iter(refs[9:])
        kernel(shape, *fixed, *[next(given) if k else None for k in kept])

    vmem, anywhere = pl.BlockSpec(memory_space=pltpu.VMEM), pl.BlockSpec(memory_space=pl.ANY)
    out = pl.pallas_call(
        body,
        out_shape=jax.ShapeDtypeStruct((height, block if scatter else width), F32),
        in_specs=[vmem] * 3 + [anywhere] * 5,
        out_specs=vmem,
        scratch_shapes=[s for s in scratch if s is not None],
        compiler_params=pltpu.CompilerParams(
            collective_id=0, has_side_effects=True, vmem_limit_bytes=62 * 1024 * 1024
        ),
        name="attribution",
    )(positions[None], donors[None], encoder_bias, context, targets, beyond_targets, encoder, decoder)
    if not scatter:
        quadrature = lax.psum_scatter(out, ("feat", "path"), scatter_dimension=1, tiled=True)
        ctxb = lax.dynamic_slice_in_dim(context[0], me * block, block, 1)
        offset = ctxb[positions].astype(F32) - ctxb[donors].astype(F32)
        out = offset * quadrature / points
    return out[None]


def solution(mesh):
    shape = tuple(mesh.shape[a] for a in ("layer", "feat", "path"))
    placed = (
        P("layer", None, None),
        P("layer", None, None),
        P(),
        P(),
        P(),
        P("layer", None, "feat"),
        P("layer", "feat"),
        P("layer", None, "feat", "path"),
    )
    return jax.shard_map(
        functools.partial(per_device, shape),
        mesh=mesh,
        in_specs=placed,
        out_specs=P("layer", None, ("feat", "path")),
        check_vma=False,
    )
```

```python
import functools

import jax
import jax.numpy as jnp
from jax import lax
from jax.experimental import pallas as pl
from jax.experimental.pallas import tpu as pltpu
from jax.sharding import PartitionSpec as P

PTS_DEV = 4
LAG = 3
MEET_GRADS = ()
MESH = pl.DeviceIdType.MESH
NT = (((1,), (1,)), ((), ()))
F32, BF16 = jnp.float32, jnp.bfloat16


def tile_of(width, most):
    sizes = [t for t in range(128, most + 1, 128) if width % t == 0]
    return sizes[-1] if sizes else width


def aligned(start, size):
    return pl.ds(pl.multiple_of(start, size), size)


def chunk_of(cols):
    return 128 if cols % 128 == 0 else cols


def decode_tiles(ncol):
    tiles, at = [], 0
    while at < ncol:
        take = min(2 if at == 0 else 4, ncol - at)
        if ncol - at - take == 1:
            take = min(3, ncol - at)
        if ncol - at == 3:
            take = 3
        tiles.append((at, take))
        at += take
    return tiles


def sent_bands(ncol):
    bands = []
    for i, (start, take) in enumerate(decode_tiles(ncol)):
        at = start
        while at < start + take:
            size = 1 if i == 0 or at + 1 == start + take else 2
            bands.append((at, size, i))
            at += size
    return bands


def kernel(
    shape, pos_ref, don_ref, bias_ref, ctx_hbm, tgt_hbm, bey_hbm, enc_hbm, dec_hbm, out_ref,
    enc, dec, ctx, table, inputs, codes, own, away, away_in, goal, send, recv, err, gsum, part, offsets, final_send, final_recv,
    enc_sem, dec_sem, load_sem, part_sem, in_send, in_recv, err_sem, back_sem, final_sem,
):
    layers, n, paths = shape
    layer, z, path = lax.axis_index("layer"), lax.axis_index("feat"), lax.axis_index("path")
    last = layers - 1
    height, tokens = pos_ref.shape[1], ctx.shape[0]
    rows, width = inputs.shape
    feats, cols = codes.shape[1], dec.shape[2]
    points = rows // height
    half = rows // 2
    cw = chunk_of(cols)
    ncol = cols // cw
    tiles, bands = decode_tiles(ncol), sent_bands(ncol)
    groups = n * paths
    me = z * paths + path
    scatter = final_send is not None

    first = jnp.where(layer == last, 1, lax.rem(layer, 2))
    second = 1 - first
    at_end = (layer == 0) | (layer == last)

    def has_neighbour(k):
        return jnp.where(k == 0, layer > 0, layer < last)

    def neighbour(k):
        return lax.rem(layer + 2 * k - 1 + layers, layers)

    low = n // 2
    upward = z < low
    depth = jnp.where(upward, z, n - 1 - z)
    to_meet = jnp.where(upward, low, n - low) - 1 - depth
    outermost, meets = depth == 0, to_meet == 0
    inner = lax.rem(jnp.where(upward, z + 1, z - 1 + n), n)
    outer = lax.rem(jnp.where(upward, z - 1 + n, z + 1), n)

    barrier = pltpu.get_barrier_semaphore()

    def greet(i, carry):
        pl.semaphore_signal(barrier, inc=1, device_id={"path": lax.rem(path + 1 + i, paths)}, device_id_type=MESH)
        return carry

    lax.fori_loop(0, paths - 1, greet, 0)

    @pl.when(z > 0)
    def _():
        pl.semaphore_signal(barrier, inc=1, device_id={"feat": z - 1}, device_id_type=MESH)

    @pl.when(z < n - 1)
    def _():
        pl.semaphore_signal(barrier, inc=1, device_id={"feat": z + 1}, device_id_type=MESH)

    @pl.when(layer > 0)
    def _():
        pl.semaphore_signal(barrier, inc=1, device_id={"layer": layer - 1}, device_id_type=MESH)

    @pl.when(layer < last)
    def _():
        pl.semaphore_signal(barrier, inc=1, device_id={"layer": layer + 1}, device_id_type=MESH)

    etile = tile_of(feats, 512)
    etiles = feats // etile
    ftile = tile_of(feats, 1024)
    ftiles = feats // ftile

    def enc_copy(j):
        return pltpu.make_async_copy(
            enc_hbm.at[0, :, aligned(j * etile, etile)], enc.at[:, aligned(j * etile, etile)], enc_sem.at[j]
        )

    def columns(at, take):
        return slice(None) if ncol == 1 else pl.ds(pl.multiple_of(at * cw, cw), take * cw)

    def dec_copy(k, i):
        at = columns(*tiles[i])
        return pltpu.make_async_copy(dec_hbm.at[0, k, :, at], dec.at[k, :, at], dec_sem.at[k, i])

    ctx_copy = pltpu.make_async_copy(ctx_hbm.at[0], ctx, load_sem.at[0])
    goal_at = slice(None) if tgt_hbm.shape[2] == cols else aligned(path * cols, cols)
    goal_copies = [
        pltpu.make_async_copy(tgt_hbm.at[0, :, goal_at], table.at[0], load_sem.at[1]),
        pltpu.make_async_copy(bey_hbm.at[:, goal_at], table.at[1], load_sem.at[2]),
    ]

    ctx_copy.start()
    for j in range(etiles):
        enc_copy(j).start()
    for copy in goal_copies:
        copy.start()

    token = lax.broadcasted_iota(jnp.int32, (tokens, height), 0)
    pick_source = (token == pos_ref[...]).astype(F32).T.astype(BF16)
    pick_donor = (token == don_ref[...]).astype(F32).T.astype(BF16)

    def pick(which, rows_of):
        return jnp.dot(which, rows_of, preferred_element_type=F32)

    ctx_copy.wait()
    donor = pick(pick_donor, ctx[...])
    offset = pick(pick_source, ctx[...]) - donor
    for p in range(points):
        inputs[p * height : (p + 1) * height, :] = (donor + ((p + 0.5) / points) * offset).astype(BF16)

    def encode(j, carry):
        enc_copy(j).wait()

        @pl.when(j == max(etiles - 2, 0))
        def _():
            for i in range(len(tiles)):
                for k in (first, second):
                    dec_copy(k, i).start()

        at = aligned(j * etile, etile)
        preact = jnp.dot(inputs[...], enc[:, at], preferred_element_type=F32) + bias_ref[:, at]
        codes[:, at] = jnp.maximum(preact, 0.0).astype(BF16)
        return carry

    lax.fori_loop(0, etiles, encode, 0)

    for copy in goal_copies:
        copy.wait()
    for k in (0, 1):
        value = pick(pick_source, table[k])
        value = jnp.where((z == low - 1) & ((k == 0) | (layer == last)), value, 0.0)
        for m in range(ncol):
            goal[k, m] = value[:, m * cw : (m + 1) * cw]

    around = jnp.minimum(z, 1) + jnp.minimum(n - 1 - z, 1) + jnp.minimum(layer, 1) + jnp.minimum(last - layer, 1)
    pl.semaphore_wait(barrier, paths - 1 + around)

    def half_rows(h):
        return aligned(h * half, half)

    def part_copy(k, i):
        at = pl.ds(*tiles[i])
        return pltpu.make_async_remote_copy(
            away.at[k, at], away_in.at[1 - k, at], part_sem.at[0, k, i], part_sem.at[1, 1 - k, i],
            device_id={"layer": neighbour(k)}, device_id_type=MESH,
        )

    def part_arrival(k, i):
        at = pl.ds(*tiles[i])
        return pltpu.make_async_remote_copy(
            away.at[k, at], away_in.at[k, at], part_sem.at[0, k, i], part_sem.at[1, k, i],
            device_id={"layer": neighbour(k)}, device_id_type=MESH,
        )

    def decode(k, i):
        dec_copy(k, i).wait()
        start, take = tiles[i]
        value = jnp.dot(codes[...], dec[k, :, columns(start, take)], preferred_element_type=F32)
        for c in range(take):
            here = value[:, c * cw : (c + 1) * cw].reshape(points, height, cw) - goal[k, start + c][None]
            own[k, start + c] = here.reshape(rows, cw)

        @pl.when(has_neighbour(k))
        def _():
            for c in range(take):
                away[k, start + c] = own[k, start + c, half_rows(k)].astype(BF16)
            part_copy(k, i).start()

    def place(k, g, whole):
        at, take, _ = bands[g]
        return pl.ds(at, take), slice(None) if whole else half_rows(1 - k)

    def in_copy(k, g, whole):
        at = place(k, g, whole)
        kind = jnp.where(meets, 1, 0)
        return pltpu.make_async_remote_copy(
            send.at[k, *at], recv.at[kind, k, *at], in_send.at[k, g], in_recv.at[kind, k, g],
            device_id={"feat": inner}, device_id_type=MESH,
        )

    def in_arrival(kind, k, g, whole):
        at = place(k, g, whole)
        return pltpu.make_async_remote_copy(
            send.at[k, *at], recv.at[kind, k, *at], in_send.at[k, g], in_recv.at[kind, k, g],
            device_id={"feat": inner}, device_id_type=MESH,
        )

    def err_copy(k, g, whole):
        at = place(k, g, whole)
        return pltpu.make_async_remote_copy(
            err.at[k, *at], err.at[k, *at], err_sem.at[0, k, g], err_sem.at[1, k, g],
            device_id={"feat": outer}, device_id_type=MESH,
        )

    def back_copy(k, g):
        at = place(k, g, False)
        return pltpu.make_async_remote_copy(
            err.at[k, *at], err.at[1 - k, *at], back_sem.at[0, k, g], back_sem.at[1, 1 - k, g],
            device_id={"layer": neighbour(k)}, device_id_type=MESH,
        )

    def back_arrival(k, g):
        at = place(1 - k, g, False)
        return pltpu.make_async_remote_copy(
            err.at[1 - k, *at], err.at[k, *at], back_sem.at[0, k, g], back_sem.at[1, k, g],
            device_id={"layer": neighbour(k)}, device_id_type=MESH,
        )

    def inward(k, g, whole, outermost):
        at = place(k, g, whole)
        base = own[k, *at]
        if not whole:
            tile = bands[g][2]
            if bands[g][0] == tiles[tile][0]:
                part_arrival(k, tile).wait_recv()
            base = base + away_in[k, at[0]].astype(F32)
        if not outermost:
            in_arrival(0, k, g, whole).wait_recv()
            base = base + recv[0, k, *at].astype(F32)
        send[k, *at] = base.astype(BF16)
        in_copy(k, g, whole).start()

    def finish(k, g, whole, meets, outermost):
        at = place(k, g, whole)
        if meets:
            in_arrival(1, k, g, whole).wait_recv()
            err[k, *at] = (send[k, *at].astype(F32) + recv[1, k, *at].astype(F32)).astype(BF16)
        else:
            err_copy(k, g, whole).wait_recv()
        if not outermost:
            err_copy(k, g, whole).start()
        if not whole:
            back_copy(k, g).start()

    def grads_step(k, gs):
        units = [u for g in gs for u in range(bands[g][0], bands[g][0] + bands[g][1])]
        here = columns(units[0], len(units))

        def of_tile(j, carry):
            f_at = aligned(j * ftile, ftile)
            errors = jnp.concatenate([err[k, u] for u in units], axis=1)
            grads = lax.dot_general(errors, dec[k, f_at, here], NT, preferred_element_type=F32)
            gated = jnp.where(codes[:, f_at].astype(F32) > 0, grads, 0.0)
            gsum[:, f_at] += gated.reshape(points, height, ftile).sum(axis=0)
            return carry

        lax.fori_loop(0, ftiles, of_tile, 0)

    gsum[...] = jnp.zeros_like(gsum)

    count = len(tiles)
    of_tile = [[g for g in range(len(bands)) if bands[g][2] == i] for i in range(count)] + [[]]
    order, step_of = [], []
    for i in range(count + 1):
        order += [(0, g) for g in of_tile[i]] + [(1, g) for g in (of_tile[i - 1] if i else [])]
        step_of += [i] * (len(order) - len(step_of))
    together = [of_tile[0]] + [[g] for i in range(1, count) for g in of_tile[i]]
    all_grads = [(s, gs) for gs in together for s in (0, 1)]

    def band(act, s, g, is_end=None):
        if s:
            act(second, g, False)
        elif is_end is None:
            pl.when(at_end)(lambda: act(first, g, True))
            pl.when(~at_end)(lambda: act(first, g, False))
        else:
            act(first, g, is_end)

    def run_grads(s, gs):
        def arrive(k):
            for g in gs:
                back_arrival(k, g).wait_recv()

        if s:
            arrive(second)
        else:
            pl.when(~at_end)(lambda: arrive(first))
        grads_step(second if s else first, gs)

    def role(meets, outermost):
        push = functools.partial(inward, outermost=outermost)
        pull = functools.partial(finish, meets=meets, outermost=outermost)
        ahead = min(LAG, len(order)) if meets else len(order)

        def start(is_end):
            at = 0
            for i in range(count):
                for s in (0, 1):
                    decode(second if s else first, i)
                    if is_end and s == (1 if meets else 0):
                        limit = i - 1 if meets else i
                        while at < ahead and step_of[at] <= limit:
                            band(push, *order[at], is_end)
                            at += 1
            for item in order[at:ahead]:
                band(push, *item, is_end)

        pl.when(at_end)(lambda: start(True))
        pl.when(~at_end)(lambda: start(False))
        left = list(all_grads)
        for j, item in enumerate(order):
            if j + ahead < len(order):
                band(push, *order[j + ahead])
            band(pull, *item)
            if not meets or j in MEET_GRADS:
                ready = [x for x in left if all((x[0], g) in order[: max(j - 1, 0)] for g in x[1])]
                for x in ready[: 1 if meets else None]:
                    run_grads(*x)
                    left.remove(x)
        for x in left:
            run_grads(*x)

    if low == 1:
        role(True, True)
    else:
        pl.when(meets)(lambda: role(True, False))
        pl.when(outermost)(lambda: role(False, True))
        if n > 4:
            pl.when(~meets & ~outermost)(lambda: role(False, False))

    if scatter:
        block = width // groups
        gated_sum = gsum[...].astype(BF16)

        def final_copy(sender, target):
            return pltpu.make_async_remote_copy(
                final_send.at[target], final_recv.at[sender], final_sem.at[0, target], final_sem.at[1, sender],
                device_id={"feat": target // paths, "path": lax.rem(target, paths)}, device_id_type=MESH,
            )

        side = groups // 2

        def send_side(i, carry):
            which = jnp.where(2 * z < n, 1 - i, i)
            at = aligned(which * side * block, side * block)
            product = lax.dot_general(gated_sum, enc[at, :], NT, preferred_element_type=F32)
            for c in range(side):
                b = which * side + c
                value = product[:, c * block : (c + 1) * block]

                @pl.when(b == me)
                def _():
                    part[...] = value

                @pl.when(b != me)
                def _():
                    final_send[b] = value.astype(BF16)
                    final_copy(me, b).start()

            return carry

        lax.fori_loop(0, 2, send_side, 0)
        for b in range(groups):
            offsets[b] = offset[:, b * block : (b + 1) * block]

        def take_block(i, carry):
            b = lax.rem(me + 1 + i, groups)
            final_copy(b, b).wait_recv()
            part[...] += final_recv[b].astype(F32)
            return carry

        lax.fori_loop(0, groups - 1, take_block, 0)
        out_ref[...] = offsets[me] * part[...] / points

        def sent_block(i, carry):
            b = lax.rem(me + 1 + i, groups)
            final_copy(me, b).wait_send()
            return carry

        lax.fori_loop(0, groups - 1, sent_block, 0)
    else:
        out_ref[...] = lax.dot_general(gsum[...].astype(BF16), enc[...], NT, preferred_element_type=F32)

    for i in range(len(tiles)):
        for k in (0, 1):

            @pl.when(has_neighbour(k))
            def _():
                part_copy(k, i).wait_send()

    def sent(k, g, whole):
        in_copy(k, g, whole).wait_send()

        @pl.when(~outermost)
        def _():
            err_copy(k, g, whole).wait_send()

        if not whole:
            back_copy(k, g).wait_send()

    for s, g in order:
        band(sent, s, g)


def per_device(shape, context, targets, beyond_targets, positions, donors, encoder, encoder_bias, decoder):
    layers, n, paths = shape
    path = lax.axis_index("path")
    height = positions.shape[0]
    tokens = context.shape[1]
    width, feats = encoder.shape[1:]
    cols = decoder.shape[3]
    points = PTS_DEV * paths
    rows = points * height
    half = rows // 2
    groups = n * paths
    block = width // groups
    me = lax.axis_index("feat") * paths + path
    scatter = block % 16 == 0 and groups % 2 == 0
    if cols % 128:
        targets = lax.dynamic_slice_in_dim(targets, path * cols, cols, 2)
        beyond_targets = lax.dynamic_slice_in_dim(beyond_targets, path * cols, cols, 1)
    dma = pltpu.SemaphoreType.DMA
    cw = chunk_of(cols)
    ncol = cols // cw
    tiles, bands = len(decode_tiles(ncol)), len(sent_bands(ncol))
    final = (
        [
            pltpu.VMEM((height, block), F32),
            pltpu.VMEM((groups, height, block), F32),
            pltpu.VMEM((groups, height, block), BF16),
            pltpu.VMEM((groups, height, block), BF16),
        ]
        if scatter
        else [None, None, None, None]
    )
    scratch = [
        pltpu.VMEM((width, feats), BF16),
        pltpu.VMEM((2, feats, cols), BF16),
        pltpu.VMEM((tokens, width), BF16),
        pltpu.VMEM((2, tokens, cols), BF16),
        pltpu.VMEM((rows, width), BF16),
        pltpu.VMEM((rows, feats), BF16),
        pltpu.VMEM((2, ncol, rows, cw), F32),
        pltpu.VMEM((2, ncol, half, cw), BF16),
        pltpu.VMEM((2, ncol, half, cw), BF16),
        pltpu.VMEM((2, ncol, height, cw), F32),
        pltpu.VMEM((2, ncol, rows, cw), BF16),
        pltpu.VMEM((2, 2, ncol, rows, cw), BF16),
        pltpu.VMEM((2, ncol, rows, cw), BF16),
        pltpu.VMEM((height, feats), F32),
        *final,
        dma((feats // tile_of(feats, 512),)),
        dma((2, tiles)),
        dma((3,)),
        dma((2, 2, tiles)),
        dma((2, bands)),
        dma((2, 2, bands)),
        dma((2, 2, bands)),
        dma((2, 2, bands)),
        dma((2, groups)) if scatter else None,
    ]
    kept = [s is not None for s in scratch]

    def body(*refs):
        fixed, given = refs[:9], iter(refs[9:])
        kernel(shape, *fixed, *[next(given) if k else None for k in kept])

    vmem, anywhere = pl.BlockSpec(memory_space=pltpu.VMEM), pl.BlockSpec(memory_space=pl.ANY)
    out = pl.pallas_call(
        body,
        out_shape=jax.ShapeDtypeStruct((height, block if scatter else width), F32),
        in_specs=[vmem] * 3 + [anywhere] * 5,
        out_specs=vmem,
        scratch_shapes=[s for s in scratch if s is not None],
        compiler_params=pltpu.CompilerParams(
            collective_id=0, has_side_effects=True, vmem_limit_bytes=62 * 1024 * 1024
        ),
        name="attribution",
    )(positions[None], donors[None], encoder_bias, context, targets, beyond_targets, encoder, decoder)
    if not scatter:
        quadrature = lax.psum_scatter(out, ("feat", "path"), scatter_dimension=1, tiled=True)
        ctxb = lax.dynamic_slice_in_dim(context[0], me * block, block, 1)
        offset = ctxb[positions].astype(F32) - ctxb[donors].astype(F32)
        out = offset * quadrature / points
    return out[None]


def solution(mesh):
    shape = tuple(mesh.shape[a] for a in ("layer", "feat", "path"))
    placed = (
        P("layer", None, None),
        P("layer", None, None),
        P(),
        P(),
        P(),
        P("layer", None, "feat"),
        P("layer", "feat"),
        P("layer", None, "feat", "path"),
    )
    return jax.shard_map(
        functools.partial(per_device, shape),
        mesh=mesh,
        in_specs=placed,
        out_specs=P("layer", None, ("feat", "path")),
        check_vma=False,
    )
```

```python
import functools

import jax
import jax.numpy as jnp
from jax import lax
from jax.experimental import pallas as pl
from jax.experimental.pallas import tpu as pltpu
from jax.sharding import PartitionSpec as P

PTS_DEV = 4
LAG = 3
MEET_GRADS = (7, 8, 9)
MESH = pl.DeviceIdType.MESH
NT = (((1,), (1,)), ((), ()))
F32, BF16 = jnp.float32, jnp.bfloat16


def tile_of(width, most):
    sizes = [t for t in range(128, most + 1, 128) if width % t == 0]
    return sizes[-1] if sizes else width


def aligned(start, size):
    return pl.ds(pl.multiple_of(start, size), size)


def chunk_of(cols):
    return 128 if cols % 128 == 0 else cols


def decode_tiles(ncol):
    tiles, at = [], 0
    while at < ncol:
        take = min(2 if at == 0 else 4, ncol - at)
        if ncol - at - take == 1:
            take = min(3, ncol - at)
        if ncol - at == 3:
            take = 3
        tiles.append((at, take))
        at += take
    return tiles


def sent_bands(ncol):
    bands = []
    for i, (start, take) in enumerate(decode_tiles(ncol)):
        at = start
        while at < start + take:
            size = 1 if i == 0 or at + 1 == start + take else 2
            bands.append((at, size, i))
            at += size
    return bands


def kernel(
    shape, pos_ref, don_ref, bias_ref, ctx_hbm, tgt_hbm, bey_hbm, enc_hbm, dec_hbm, out_ref,
    enc, dec, ctx, table, inputs, codes, own, away, away_in, goal, send, recv, err, gsum, part, offsets, final_send, final_recv,
    enc_sem, dec_sem, load_sem, part_sem, in_send, in_recv, err_sem, back_sem, final_sem,
):
    layers, n, paths = shape
    layer, z, path = lax.axis_index("layer"), lax.axis_index("feat"), lax.axis_index("path")
    last = layers - 1
    height, tokens = pos_ref.shape[1], ctx.shape[0]
    rows, width = inputs.shape
    feats, cols = codes.shape[1], dec.shape[2]
    points = rows // height
    half = rows // 2
    cw = chunk_of(cols)
    ncol = cols // cw
    tiles, bands = decode_tiles(ncol), sent_bands(ncol)
    groups = n * paths
    me = z * paths + path
    scatter = final_send is not None

    first = jnp.where(layer == last, 1, lax.rem(layer, 2))
    second = 1 - first
    at_end = (layer == 0) | (layer == last)

    def has_neighbour(k):
        return jnp.where(k == 0, layer > 0, layer < last)

    def neighbour(k):
        return lax.rem(layer + 2 * k - 1 + layers, layers)

    low = n // 2
    upward = z < low
    depth = jnp.where(upward, z, n - 1 - z)
    to_meet = jnp.where(upward, low, n - low) - 1 - depth
    outermost, meets = depth == 0, to_meet == 0
    inner = lax.rem(jnp.where(upward, z + 1, z - 1 + n), n)
    outer = lax.rem(jnp.where(upward, z - 1 + n, z + 1), n)

    barrier = pltpu.get_barrier_semaphore()

    def greet(i, carry):
        pl.semaphore_signal(barrier, inc=1, device_id={"path": lax.rem(path + 1 + i, paths)}, device_id_type=MESH)
        return carry

    lax.fori_loop(0, paths - 1, greet, 0)

    @pl.when(z > 0)
    def _():
        pl.semaphore_signal(barrier, inc=1, device_id={"feat": z - 1}, device_id_type=MESH)

    @pl.when(z < n - 1)
    def _():
        pl.semaphore_signal(barrier, inc=1, device_id={"feat": z + 1}, device_id_type=MESH)

    @pl.when(layer > 0)
    def _():
        pl.semaphore_signal(barrier, inc=1, device_id={"layer": layer - 1}, device_id_type=MESH)

    @pl.when(layer < last)
    def _():
        pl.semaphore_signal(barrier, inc=1, device_id={"layer": layer + 1}, device_id_type=MESH)

    etile = tile_of(feats, 512)
    etiles = feats // etile
    ftile = tile_of(feats, 1024)
    ftiles = feats // ftile

    def enc_copy(j):
        return pltpu.make_async_copy(
            enc_hbm.at[0, :, aligned(j * etile, etile)], enc.at[:, aligned(j * etile, etile)], enc_sem.at[j]
        )

    def columns(at, take):
        return slice(None) if ncol == 1 else pl.ds(pl.multiple_of(at * cw, cw), take * cw)

    def dec_copy(k, i):
        at = columns(*tiles[i])
        return pltpu.make_async_copy(dec_hbm.at[0, k, :, at], dec.at[k, :, at], dec_sem.at[k, i])

    ctx_copy = pltpu.make_async_copy(ctx_hbm.at[0], ctx, load_sem.at[0])
    goal_at = slice(None) if tgt_hbm.shape[2] == cols else aligned(path * cols, cols)
    goal_copies = [
        pltpu.make_async_copy(tgt_hbm.at[0, :, goal_at], table.at[0], load_sem.at[1]),
        pltpu.make_async_copy(bey_hbm.at[:, goal_at], table.at[1], load_sem.at[2]),
    ]

    ctx_copy.start()
    for j in range(etiles):
        enc_copy(j).start()
    for copy in goal_copies:
        copy.start()

    token = lax.broadcasted_iota(jnp.int32, (tokens, height), 0)
    pick_source = (token == pos_ref[...]).astype(F32).T.astype(BF16)
    pick_donor = (token == don_ref[...]).astype(F32).T.astype(BF16)

    def pick(which, rows_of):
        return jnp.dot(which, rows_of, preferred_element_type=F32)

    ctx_copy.wait()
    donor = pick(pick_donor, ctx[...])
    offset = pick(pick_source, ctx[...]) - donor
    for p in range(points):
        inputs[p * height : (p + 1) * height, :] = (donor + ((p + 0.5) / points) * offset).astype(BF16)

    def encode(j, carry):
        enc_copy(j).wait()

        @pl.when(j == max(etiles - 2, 0))
        def _():
            for i in range(len(tiles)):
                for k in (first, second):
                    dec_copy(k, i).start()

        at = aligned(j * etile, etile)
        preact = jnp.dot(inputs[...], enc[:, at], preferred_element_type=F32) + bias_ref[:, at]
        codes[:, at] = jnp.maximum(preact, 0.0).astype(BF16)
        return carry

    lax.fori_loop(0, etiles, encode, 0)

    for copy in goal_copies:
        copy.wait()
    for k in (0, 1):
        value = pick(pick_source, table[k])
        value = jnp.where((z == low - 1) & ((k == 0) | (layer == last)), value, 0.0)
        for m in range(ncol):
            goal[k, m] = value[:, m * cw : (m + 1) * cw]

    around = jnp.minimum(z, 1) + jnp.minimum(n - 1 - z, 1) + jnp.minimum(layer, 1) + jnp.minimum(last - layer, 1)
    pl.semaphore_wait(barrier, paths - 1 + around)

    def half_rows(h):
        return aligned(h * half, half)

    def part_copy(k, i):
        at = pl.ds(*tiles[i])
        return pltpu.make_async_remote_copy(
            away.at[k, at], away_in.at[1 - k, at], part_sem.at[0, k, i], part_sem.at[1, 1 - k, i],
            device_id={"layer": neighbour(k)}, device_id_type=MESH,
        )

    def part_arrival(k, i):
        at = pl.ds(*tiles[i])
        return pltpu.make_async_remote_copy(
            away.at[k, at], away_in.at[k, at], part_sem.at[0, k, i], part_sem.at[1, k, i],
            device_id={"layer": neighbour(k)}, device_id_type=MESH,
        )

    def decode(k, i):
        dec_copy(k, i).wait()
        start, take = tiles[i]
        value = jnp.dot(codes[...], dec[k, :, columns(start, take)], preferred_element_type=F32)
        for c in range(take):
            here = value[:, c * cw : (c + 1) * cw].reshape(points, height, cw) - goal[k, start + c][None]
            own[k, start + c] = here.reshape(rows, cw)

        @pl.when(has_neighbour(k))
        def _():
            for c in range(take):
                away[k, start + c] = own[k, start + c, half_rows(k)].astype(BF16)
            part_copy(k, i).start()

    def place(k, g, whole):
        at, take, _ = bands[g]
        return pl.ds(at, take), slice(None) if whole else half_rows(1 - k)

    def in_copy(k, g, whole):
        at = place(k, g, whole)
        kind = jnp.where(meets, 1, 0)
        return pltpu.make_async_remote_copy(
            send.at[k, *at], recv.at[kind, k, *at], in_send.at[k, g], in_recv.at[kind, k, g],
            device_id={"feat": inner}, device_id_type=MESH,
        )

    def in_arrival(kind, k, g, whole):
        at = place(k, g, whole)
        return pltpu.make_async_remote_copy(
            send.at[k, *at], recv.at[kind, k, *at], in_send.at[k, g], in_recv.at[kind, k, g],
            device_id={"feat": inner}, device_id_type=MESH,
        )

    def err_copy(k, g, whole):
        at = place(k, g, whole)
        return pltpu.make_async_remote_copy(
            err.at[k, *at], err.at[k, *at], err_sem.at[0, k, g], err_sem.at[1, k, g],
            device_id={"feat": outer}, device_id_type=MESH,
        )

    def back_copy(k, g):
        at = place(k, g, False)
        return pltpu.make_async_remote_copy(
            err.at[k, *at], err.at[1 - k, *at], back_sem.at[0, k, g], back_sem.at[1, 1 - k, g],
            device_id={"layer": neighbour(k)}, device_id_type=MESH,
        )

    def back_arrival(k, g):
        at = place(1 - k, g, False)
        return pltpu.make_async_remote_copy(
            err.at[1 - k, *at], err.at[k, *at], back_sem.at[0, k, g], back_sem.at[1, k, g],
            device_id={"layer": neighbour(k)}, device_id_type=MESH,
        )

    def inward(k, g, whole, outermost):
        at = place(k, g, whole)
        base = own[k, *at]
        if not whole:
            tile = bands[g][2]
            if bands[g][0] == tiles[tile][0]:
                part_arrival(k, tile).wait_recv()
            base = base + away_in[k, at[0]].astype(F32)
        if not outermost:
            in_arrival(0, k, g, whole).wait_recv()
            base = base + recv[0, k, *at].astype(F32)
        send[k, *at] = base.astype(BF16)
        in_copy(k, g, whole).start()

    def finish(k, g, whole, meets, outermost):
        at = place(k, g, whole)
        if meets:
            in_arrival(1, k, g, whole).wait_recv()
            err[k, *at] = (send[k, *at].astype(F32) + recv[1, k, *at].astype(F32)).astype(BF16)
        else:
            err_copy(k, g, whole).wait_recv()
        if not outermost:
            err_copy(k, g, whole).start()
        if not whole:
            back_copy(k, g).start()

    def grads_step(k, gs):
        units = [u for g in gs for u in range(bands[g][0], bands[g][0] + bands[g][1])]
        here = columns(units[0], len(units))

        def of_tile(j, carry):
            f_at = aligned(j * ftile, ftile)
            errors = jnp.concatenate([err[k, u] for u in units], axis=1)
            grads = lax.dot_general(errors, dec[k, f_at, here], NT, preferred_element_type=F32)
            gated = jnp.where(codes[:, f_at].astype(F32) > 0, grads, 0.0)
            gsum[:, f_at] += gated.reshape(points, height, ftile).sum(axis=0)
            return carry

        lax.fori_loop(0, ftiles, of_tile, 0)

    gsum[...] = jnp.zeros_like(gsum)

    count = len(tiles)
    of_tile = [[g for g in range(len(bands)) if bands[g][2] == i] for i in range(count)] + [[]]
    order, step_of = [], []
    for i in range(count + 1):
        order += [(0, g) for g in of_tile[i]] + [(1, g) for g in (of_tile[i - 1] if i else [])]
        step_of += [i] * (len(order) - len(step_of))
    together = [of_tile[0]] + [[g] for i in range(1, count) for g in of_tile[i]]
    all_grads = [(s, gs) for gs in together for s in (0, 1)]

    def band(act, s, g, is_end=None):
        if s:
            act(second, g, False)
        elif is_end is None:
            pl.when(at_end)(lambda: act(first, g, True))
            pl.when(~at_end)(lambda: act(first, g, False))
        else:
            act(first, g, is_end)

    def run_grads(s, gs):
        def arrive(k):
            for g in gs:
                back_arrival(k, g).wait_recv()

        if s:
            arrive(second)
        else:
            pl.when(~at_end)(lambda: arrive(first))
        grads_step(second if s else first, gs)

    def role(meets, outermost, stage=None):
        push = functools.partial(inward, outermost=outermost)
        pull = functools.partial(finish, meets=meets, outermost=outermost)
        ahead = min(LAG, len(order)) if meets else len(order)

        if stage is not None:
            i, s = stage
            limit = i - 1 if meets else i
            if s == (1 if meets else 0):
                for item, step in zip(order[:ahead], step_of):
                    if step == limit:
                        band(push, *item, True)
            return

        def start(is_end):
            for item, step in zip(order[:ahead], step_of):
                if not is_end or step > count - (2 if meets else 1):
                    band(push, *item, is_end)

        pl.when(at_end)(lambda: start(True))
        pl.when(~at_end)(lambda: start(False))
        left = list(all_grads)
        for j, item in enumerate(order):
            if j + ahead < len(order):
                band(push, *order[j + ahead])
            band(pull, *item)
            if not meets or j in MEET_GRADS:
                ready = [x for x in left if all((x[0], g) in order[: max(j - 1, 0)] for g in x[1])]
                for x in ready[: 1 if meets else None]:
                    run_grads(*x)
                    left.remove(x)
        for x in left:
            run_grads(*x)

    def roles(stage, allowed):
        if low == 1:
            pl.when(allowed)(lambda: role(True, True, stage))
        else:
            pl.when(meets & allowed)(lambda: role(True, False, stage))
            pl.when(outermost & allowed)(lambda: role(False, True, stage))
            if n > 4:
                pl.when(~meets & ~outermost & allowed)(lambda: role(False, False, stage))

    for i in range(count):
        for s in (0, 1):
            decode(second if s else first, i)
            roles((i, s), at_end)
    roles(None, layer >= 0)

    if scatter:
        block = width // groups
        gated_sum = gsum[...].astype(BF16)

        def final_copy(sender, target):
            return pltpu.make_async_remote_copy(
                final_send.at[target], final_recv.at[sender], final_sem.at[0, target], final_sem.at[1, sender],
                device_id={"feat": target // paths, "path": lax.rem(target, paths)}, device_id_type=MESH,
            )

        side = paths

        def send_side(i, carry):
            which = jnp.where(upward, n - 1 - i, i)
            at = aligned(which * side * block, side * block)
            product = lax.dot_general(gated_sum, enc[at, :], NT, preferred_element_type=F32)
            for c in range(side):
                b = which * side + c
                value = product[:, c * block : (c + 1) * block]

                @pl.when(b == me)
                def _():
                    part[...] = value

                @pl.when(b != me)
                def _():
                    final_send[b] = value.astype(BF16)
                    final_copy(me, b).start()

            return carry

        lax.fori_loop(0, n, send_side, 0)
        for b in range(groups):
            offsets[b] = offset[:, b * block : (b + 1) * block]

        def take_block(i, carry):
            b = lax.rem(me + 1 + i, groups)
            final_copy(b, b).wait_recv()
            part[...] += final_recv[b].astype(F32)
            return carry

        lax.fori_loop(0, groups - 1, take_block, 0)
        out_ref[...] = offsets[me] * part[...] / points

        def sent_block(i, carry):
            b = lax.rem(me + 1 + i, groups)
            final_copy(me, b).wait_send()
            return carry

        lax.fori_loop(0, groups - 1, sent_block, 0)
    else:
        out_ref[...] = lax.dot_general(gsum[...].astype(BF16), enc[...], NT, preferred_element_type=F32)

    for i in range(len(tiles)):
        for k in (0, 1):

            @pl.when(has_neighbour(k))
            def _():
                part_copy(k, i).wait_send()

    def sent(k, g, whole):
        in_copy(k, g, whole).wait_send()

        @pl.when(~outermost)
        def _():
            err_copy(k, g, whole).wait_send()

        if not whole:
            back_copy(k, g).wait_send()

    for s, g in order:
        band(sent, s, g)


def per_device(shape, context, targets, beyond_targets, positions, donors, encoder, encoder_bias, decoder):
    layers, n, paths = shape
    path = lax.axis_index("path")
    height = positions.shape[0]
    tokens = context.shape[1]
    width, feats = encoder.shape[1:]
    cols = decoder.shape[3]
    points = PTS_DEV * paths
    rows = points * height
    half = rows // 2
    groups = n * paths
    block = width // groups
    me = lax.axis_index("feat") * paths + path
    scatter = block % 16 == 0 and groups % 2 == 0
    if cols % 128:
        targets = lax.dynamic_slice_in_dim(targets, path * cols, cols, 2)
        beyond_targets = lax.dynamic_slice_in_dim(beyond_targets, path * cols, cols, 1)
    dma = pltpu.SemaphoreType.DMA
    cw = chunk_of(cols)
    ncol = cols // cw
    tiles, bands = len(decode_tiles(ncol)), len(sent_bands(ncol))
    final = (
        [
            pltpu.VMEM((height, block), F32),
            pltpu.VMEM((groups, height, block), F32),
            pltpu.VMEM((groups, height, block), BF16),
            pltpu.VMEM((groups, height, block), BF16),
        ]
        if scatter
        else [None, None, None, None]
    )
    scratch = [
        pltpu.VMEM((width, feats), BF16),
        pltpu.VMEM((2, feats, cols), BF16),
        pltpu.VMEM((tokens, width), BF16),
        pltpu.VMEM((2, tokens, cols), BF16),
        pltpu.VMEM((rows, width), BF16),
        pltpu.VMEM((rows, feats), BF16),
        pltpu.VMEM((2, ncol, rows, cw), F32),
        pltpu.VMEM((2, ncol, half, cw), BF16),
        pltpu.VMEM((2, ncol, half, cw), BF16),
        pltpu.VMEM((2, ncol, height, cw), F32),
        pltpu.VMEM((2, ncol, rows, cw), BF16),
        pltpu.VMEM((2, 2, ncol, rows, cw), BF16),
        pltpu.VMEM((2, ncol, rows, cw), BF16),
        pltpu.VMEM((height, feats), F32),
        *final,
        dma((feats // tile_of(feats, 512),)),
        dma((2, tiles)),
        dma((3,)),
        dma((2, 2, tiles)),
        dma((2, bands)),
        dma((2, 2, bands)),
        dma((2, 2, bands)),
        dma((2, 2, bands)),
        dma((2, groups)) if scatter else None,
    ]
    kept = [s is not None for s in scratch]

    def body(*refs):
        fixed, given = refs[:9], iter(refs[9:])
        kernel(shape, *fixed, *[next(given) if k else None for k in kept])

    vmem, anywhere = pl.BlockSpec(memory_space=pltpu.VMEM), pl.BlockSpec(memory_space=pl.ANY)
    out = pl.pallas_call(
        body,
        out_shape=jax.ShapeDtypeStruct((height, block if scatter else width), F32),
        in_specs=[vmem] * 3 + [anywhere] * 5,
        out_specs=vmem,
        scratch_shapes=[s for s in scratch if s is not None],
        compiler_params=pltpu.CompilerParams(
            collective_id=0, has_side_effects=True, vmem_limit_bytes=62 * 1024 * 1024
        ),
        name="attribution",
    )(positions[None], donors[None], encoder_bias, context, targets, beyond_targets, encoder, decoder)
    if not scatter:
        quadrature = lax.psum_scatter(out, ("feat", "path"), scatter_dimension=1, tiled=True)
        ctxb = lax.dynamic_slice_in_dim(context[0], me * block, block, 1)
        offset = ctxb[positions].astype(F32) - ctxb[donors].astype(F32)
        out = offset * quadrature / points
    return out[None]


def solution(mesh):
    shape = tuple(mesh.shape[a] for a in ("layer", "feat", "path"))
    placed = (
        P("layer", None, None),
        P("layer", None, None),
        P(),
        P(),
        P(),
        P("layer", None, "feat"),
        P("layer", "feat"),
        P("layer", None, "feat", "path"),
    )
    return jax.shard_map(
        functools.partial(per_device, shape),
        mesh=mesh,
        in_specs=placed,
        out_specs=P("layer", None, ("feat", "path")),
        check_vma=False,
    )
```

```python
import functools

import jax
import jax.numpy as jnp
from jax import lax
from jax.experimental import pallas as pl
from jax.experimental.pallas import tpu as pltpu
from jax.sharding import PartitionSpec as P

PTS_DEV = 4
LAG = 3
MEET_GRADS = (7, 8, 9)
MESH = pl.DeviceIdType.MESH
NT = (((1,), (1,)), ((), ()))
F32, BF16 = jnp.float32, jnp.bfloat16


def tile_of(width, most):
    sizes = [t for t in range(128, most + 1, 128) if width % t == 0]
    return sizes[-1] if sizes else width


def aligned(start, size):
    return pl.ds(pl.multiple_of(start, size), size)


def chunk_of(cols):
    return 128 if cols % 128 == 0 else cols


def decode_tiles(ncol):
    tiles, at = [], 0
    while at < ncol:
        take = min(2 if at == 0 else 4, ncol - at)
        if ncol - at - take == 1:
            take = min(3, ncol - at)
        if ncol - at == 3:
            take = 3
        tiles.append((at, take))
        at += take
    return tiles


def sent_bands(ncol):
    bands = []
    for i, (start, take) in enumerate(decode_tiles(ncol)):
        at = start
        while at < start + take:
            size = 1 if i == 0 or at + 1 == start + take else 2
            bands.append((at, size, i))
            at += size
    return bands


def kernel(
    shape, pos_ref, don_ref, bias_ref, ctx_hbm, tgt_hbm, bey_hbm, enc_hbm, dec_hbm, out_ref,
    enc, dec, ctx, table, inputs, codes, own, away, away_in, goal, send, recv, err, gsum, part, offsets, final_send, final_recv,
    enc_sem, dec_sem, load_sem, part_sem, in_send, in_recv, err_sem, back_sem, final_sem,
):
    layers, n, paths = shape
    layer, z, path = lax.axis_index("layer"), lax.axis_index("feat"), lax.axis_index("path")
    last = layers - 1
    height, tokens = pos_ref.shape[1], ctx.shape[0]
    rows, width = inputs.shape
    feats, cols = codes.shape[1], dec.shape[2]
    points = rows // height
    half = rows // 2
    cw = chunk_of(cols)
    ncol = cols // cw
    tiles, bands = decode_tiles(ncol), sent_bands(ncol)
    groups = n * paths
    me = z * paths + path
    scatter = final_send is not None

    first = jnp.where(layer == last, 1, lax.rem(layer, 2))
    second = 1 - first
    at_end = (layer == 0) | (layer == last)

    def has_neighbour(k):
        return jnp.where(k == 0, layer > 0, layer < last)

    def neighbour(k):
        return lax.rem(layer + 2 * k - 1 + layers, layers)

    low = n // 2
    upward = z < low
    depth = jnp.where(upward, z, n - 1 - z)
    to_meet = jnp.where(upward, low, n - low) - 1 - depth
    outermost, meets = depth == 0, to_meet == 0
    inner = lax.rem(jnp.where(upward, z + 1, z - 1 + n), n)
    outer = lax.rem(jnp.where(upward, z - 1 + n, z + 1), n)

    barrier = pltpu.get_barrier_semaphore()

    def greet(i, carry):
        pl.semaphore_signal(barrier, inc=1, device_id={"path": lax.rem(path + 1 + i, paths)}, device_id_type=MESH)
        return carry

    lax.fori_loop(0, paths - 1, greet, 0)

    @pl.when(z > 0)
    def _():
        pl.semaphore_signal(barrier, inc=1, device_id={"feat": z - 1}, device_id_type=MESH)

    @pl.when(z < n - 1)
    def _():
        pl.semaphore_signal(barrier, inc=1, device_id={"feat": z + 1}, device_id_type=MESH)

    @pl.when(layer > 0)
    def _():
        pl.semaphore_signal(barrier, inc=1, device_id={"layer": layer - 1}, device_id_type=MESH)

    @pl.when(layer < last)
    def _():
        pl.semaphore_signal(barrier, inc=1, device_id={"layer": layer + 1}, device_id_type=MESH)

    etile = tile_of(feats, 512)
    etiles = feats // etile
    ftile = tile_of(feats, 2048)
    ftiles = feats // ftile

    def enc_copy(j):
        return pltpu.make_async_copy(
            enc_hbm.at[0, :, aligned(j * etile, etile)], enc.at[:, aligned(j * etile, etile)], enc_sem.at[j]
        )

    def columns(at, take):
        return slice(None) if ncol == 1 else pl.ds(pl.multiple_of(at * cw, cw), take * cw)

    def dec_copy(k, i):
        at = columns(*tiles[i])
        return pltpu.make_async_copy(dec_hbm.at[0, k, :, at], dec.at[k, :, at], dec_sem.at[k, i])

    ctx_copy = pltpu.make_async_copy(ctx_hbm.at[0], ctx, load_sem.at[0])
    goal_at = slice(None) if tgt_hbm.shape[2] == cols else aligned(path * cols, cols)
    goal_copies = [
        pltpu.make_async_copy(tgt_hbm.at[0, :, goal_at], table.at[0], load_sem.at[1]),
        pltpu.make_async_copy(bey_hbm.at[:, goal_at], table.at[1], load_sem.at[2]),
    ]

    ctx_copy.start()
    for j in range(etiles):
        enc_copy(j).start()
    for copy in goal_copies:
        copy.start()

    token = lax.broadcasted_iota(jnp.int32, (tokens, height), 0)
    pick_source = (token == pos_ref[...]).astype(F32).T.astype(BF16)
    pick_donor = (token == don_ref[...]).astype(F32).T.astype(BF16)

    def pick(which, rows_of):
        return jnp.dot(which, rows_of, preferred_element_type=F32)

    ctx_copy.wait()
    donor = pick(pick_donor, ctx[...])
    offset = pick(pick_source, ctx[...]) - donor
    for p in range(points):
        inputs[p * height : (p + 1) * height, :] = (donor + ((p + 0.5) / points) * offset).astype(BF16)

    def encode(j, carry):
        enc_copy(j).wait()

        @pl.when(j == max(etiles - 2, 0))
        def _():
            for i in range(len(tiles)):
                for k in (first, second):
                    dec_copy(k, i).start()

        at = aligned(j * etile, etile)
        preact = jnp.dot(inputs[...], enc[:, at], preferred_element_type=F32) + bias_ref[:, at]
        codes[:, at] = jnp.maximum(preact, 0.0).astype(BF16)
        return carry

    lax.fori_loop(0, etiles, encode, 0)

    for copy in goal_copies:
        copy.wait()
    for k in (0, 1):
        value = pick(pick_source, table[k])
        value = jnp.where((z == low - 1) & ((k == 0) | (layer == last)), value, 0.0)
        for m in range(ncol):
            goal[k, m] = value[:, m * cw : (m + 1) * cw]

    around = jnp.minimum(z, 1) + jnp.minimum(n - 1 - z, 1) + jnp.minimum(layer, 1) + jnp.minimum(last - layer, 1)
    pl.semaphore_wait(barrier, paths - 1 + around)

    def half_rows(h):
        return aligned(h * half, half)

    def part_copy(k, i):
        at = pl.ds(*tiles[i])
        return pltpu.make_async_remote_copy(
            away.at[k, at], away_in.at[1 - k, at], part_sem.at[0, k, i], part_sem.at[1, 1 - k, i],
            device_id={"layer": neighbour(k)}, device_id_type=MESH,
        )

    def part_arrival(k, i):
        at = pl.ds(*tiles[i])
        return pltpu.make_async_remote_copy(
            away.at[k, at], away_in.at[k, at], part_sem.at[0, k, i], part_sem.at[1, k, i],
            device_id={"layer": neighbour(k)}, device_id_type=MESH,
        )

    def decode(k, i):
        dec_copy(k, i).wait()
        start, take = tiles[i]
        value = jnp.dot(codes[...], dec[k, :, columns(start, take)], preferred_element_type=F32)
        for c in range(take):
            here = value[:, c * cw : (c + 1) * cw].reshape(points, height, cw) - goal[k, start + c][None]
            own[k, start + c] = here.reshape(rows, cw)

        @pl.when(has_neighbour(k))
        def _():
            for c in range(take):
                away[k, start + c] = own[k, start + c, half_rows(k)].astype(BF16)
            part_copy(k, i).start()

    def place(k, g, whole):
        at, take, _ = bands[g]
        return pl.ds(at, take), slice(None) if whole else half_rows(1 - k)

    def in_copy(k, g, whole):
        at = place(k, g, whole)
        kind = jnp.where(meets, 1, 0)
        return pltpu.make_async_remote_copy(
            send.at[k, *at], recv.at[kind, k, *at], in_send.at[k, g], in_recv.at[kind, k, g],
            device_id={"feat": inner}, device_id_type=MESH,
        )

    def in_arrival(kind, k, g, whole):
        at = place(k, g, whole)
        return pltpu.make_async_remote_copy(
            send.at[k, *at], recv.at[kind, k, *at], in_send.at[k, g], in_recv.at[kind, k, g],
            device_id={"feat": inner}, device_id_type=MESH,
        )

    def err_copy(k, g, whole):
        at = place(k, g, whole)
        return pltpu.make_async_remote_copy(
            err.at[k, *at], err.at[k, *at], err_sem.at[0, k, g], err_sem.at[1, k, g],
            device_id={"feat": outer}, device_id_type=MESH,
        )

    def back_copy(k, g):
        at = place(k, g, False)
        return pltpu.make_async_remote_copy(
            err.at[k, *at], err.at[1 - k, *at], back_sem.at[0, k, g], back_sem.at[1, 1 - k, g],
            device_id={"layer": neighbour(k)}, device_id_type=MESH,
        )

    def back_arrival(k, g):
        at = place(1 - k, g, False)
        return pltpu.make_async_remote_copy(
            err.at[1 - k, *at], err.at[k, *at], back_sem.at[0, k, g], back_sem.at[1, k, g],
            device_id={"layer": neighbour(k)}, device_id_type=MESH,
        )

    def inward(k, g, whole, outermost):
        at = place(k, g, whole)
        base = own[k, *at]
        if not whole:
            tile = bands[g][2]
            if bands[g][0] == tiles[tile][0]:
                part_arrival(k, tile).wait_recv()
            base = base + away_in[k, at[0]].astype(F32)
        if not outermost:
            in_arrival(0, k, g, whole).wait_recv()
            base = base + recv[0, k, *at].astype(F32)
        send[k, *at] = base.astype(BF16)
        in_copy(k, g, whole).start()

    def finish(k, g, whole, meets, outermost):
        at = place(k, g, whole)
        if meets:
            in_arrival(1, k, g, whole).wait_recv()
            err[k, *at] = (send[k, *at].astype(F32) + recv[1, k, *at].astype(F32)).astype(BF16)
        else:
            err_copy(k, g, whole).wait_recv()
        if not outermost:
            err_copy(k, g, whole).start()
        if not whole:
            back_copy(k, g).start()

    def grads_step(k, gs):
        units = [u for g in gs for u in range(bands[g][0], bands[g][0] + bands[g][1])]
        here = columns(units[0], len(units))

        def of_tile(j, carry):
            f_at = aligned(j * ftile, ftile)
            errors = jnp.concatenate([err[k, u] for u in units], axis=1)
            grads = lax.dot_general(errors, dec[k, f_at, here], NT, preferred_element_type=F32)
            gated = jnp.where(codes[:, f_at].astype(F32) > 0, grads, 0.0)
            gsum[:, f_at] += gated.reshape(points, height, ftile).sum(axis=0)
            return carry

        lax.fori_loop(0, ftiles, of_tile, 0)

    gsum[...] = jnp.zeros_like(gsum)

    count = len(tiles)
    of_tile = [[g for g in range(len(bands)) if bands[g][2] == i] for i in range(count)] + [[]]
    order, step_of = [], []
    for i in range(count + 1):
        order += [(0, g) for g in of_tile[i]] + [(1, g) for g in (of_tile[i - 1] if i else [])]
        step_of += [i] * (len(order) - len(step_of))
    together = [of_tile[0]] + [[g] for i in range(1, count) for g in of_tile[i]]
    all_grads = [(s, gs) for gs in together for s in (0, 1)]

    def band(act, s, g, is_end=None):
        if s:
            act(second, g, False)
        elif is_end is None:
            pl.when(at_end)(lambda: act(first, g, True))
            pl.when(~at_end)(lambda: act(first, g, False))
        else:
            act(first, g, is_end)

    def run_grads(s, gs):
        def arrive(k):
            for g in gs:
                back_arrival(k, g).wait_recv()

        if s:
            arrive(second)
        else:
            pl.when(~at_end)(lambda: arrive(first))
        grads_step(second if s else first, gs)

    def role(meets, outermost, stage=None):
        push = functools.partial(inward, outermost=outermost)
        pull = functools.partial(finish, meets=meets, outermost=outermost)
        ahead = min(LAG, len(order)) if meets else len(order)

        if stage is not None:
            i, s = stage
            limit = i - 1 if meets else i
            if s == (1 if meets else 0):
                for item, step in zip(order[:ahead], step_of):
                    if step == limit:
                        band(push, *item, True)
            return

        def start(is_end):
            for item, step in zip(order[:ahead], step_of):
                if not is_end or step > count - (2 if meets else 1):
                    band(push, *item, is_end)

        pl.when(at_end)(lambda: start(True))
        pl.when(~at_end)(lambda: start(False))
        left = list(all_grads)
        for j, item in enumerate(order):
            if j + ahead < len(order):
                band(push, *order[j + ahead])
            band(pull, *item)
            if not meets or j in MEET_GRADS:
                ready = [x for x in left if all((x[0], g) in order[: max(j - 1, 0)] for g in x[1])]
                for x in ready[: 1 if meets else None]:
                    run_grads(*x)
                    left.remove(x)
        for x in left:
            run_grads(*x)

    def roles(stage, allowed):
        if low == 1:
            pl.when(allowed)(lambda: role(True, True, stage))
        else:
            pl.when(meets & allowed)(lambda: role(True, False, stage))
            pl.when(outermost & allowed)(lambda: role(False, True, stage))
            if n > 4:
                pl.when(~meets & ~outermost & allowed)(lambda: role(False, False, stage))

    for i in range(count):
        for s in (0, 1):
            decode(second if s else first, i)
            roles((i, s), at_end)
    roles(None, layer >= 0)

    if scatter:
        block = width // groups
        gated_sum = gsum[...].astype(BF16)

        def final_copy(sender, target):
            return pltpu.make_async_remote_copy(
                final_send.at[target], final_recv.at[sender], final_sem.at[0, target], final_sem.at[1, sender],
                device_id={"feat": target // paths, "path": lax.rem(target, paths)}, device_id_type=MESH,
            )

        side = paths

        def send_side(i, carry):
            which = jnp.where(upward, n - 1 - i, i)
            at = aligned(which * side * block, side * block)
            product = lax.dot_general(gated_sum, enc[at, :], NT, preferred_element_type=F32)
            for c in range(side):
                b = which * side + c
                value = product[:, c * block : (c + 1) * block]

                @pl.when(b == me)
                def _():
                    part[...] = value

                @pl.when(b != me)
                def _():
                    final_send[b] = value.astype(BF16)
                    final_copy(me, b).start()

            return carry

        lax.fori_loop(0, n, send_side, 0)
        for b in range(groups):
            offsets[b] = offset[:, b * block : (b + 1) * block]

        def take_block(i, carry):
            b = lax.rem(me + 1 + i, groups)
            final_copy(b, b).wait_recv()
            part[...] += final_recv[b].astype(F32)
            return carry

        lax.fori_loop(0, groups - 1, take_block, 0)
        out_ref[...] = offsets[me] * part[...] / points

        def sent_block(i, carry):
            b = lax.rem(me + 1 + i, groups)
            final_copy(me, b).wait_send()
            return carry

        lax.fori_loop(0, groups - 1, sent_block, 0)
    else:
        out_ref[...] = lax.dot_general(gsum[...].astype(BF16), enc[...], NT, preferred_element_type=F32)

    for i in range(len(tiles)):
        for k in (0, 1):

            @pl.when(has_neighbour(k))
            def _():
                part_copy(k, i).wait_send()

    def sent(k, g, whole):
        in_copy(k, g, whole).wait_send()

        @pl.when(~outermost)
        def _():
            err_copy(k, g, whole).wait_send()

        if not whole:
            back_copy(k, g).wait_send()

    for s, g in order:
        band(sent, s, g)


def per_device(shape, context, targets, beyond_targets, positions, donors, encoder, encoder_bias, decoder):
    layers, n, paths = shape
    path = lax.axis_index("path")
    height = positions.shape[0]
    tokens = context.shape[1]
    width, feats = encoder.shape[1:]
    cols = decoder.shape[3]
    points = PTS_DEV * paths
    rows = points * height
    half = rows // 2
    groups = n * paths
    block = width // groups
    me = lax.axis_index("feat") * paths + path
    scatter = block % 16 == 0 and groups % 2 == 0
    if cols % 128:
        targets = lax.dynamic_slice_in_dim(targets, path * cols, cols, 2)
        beyond_targets = lax.dynamic_slice_in_dim(beyond_targets, path * cols, cols, 1)
    dma = pltpu.SemaphoreType.DMA
    cw = chunk_of(cols)
    ncol = cols // cw
    tiles, bands = len(decode_tiles(ncol)), len(sent_bands(ncol))
    final = (
        [
            pltpu.VMEM((height, block), F32),
            pltpu.VMEM((groups, height, block), F32),
            pltpu.VMEM((groups, height, block), BF16),
            pltpu.VMEM((groups, height, block), BF16),
        ]
        if scatter
        else [None, None, None, None]
    )
    scratch = [
        pltpu.VMEM((width, feats), BF16),
        pltpu.VMEM((2, feats, cols), BF16),
        pltpu.VMEM((tokens, width), BF16),
        pltpu.VMEM((2, tokens, cols), BF16),
        pltpu.VMEM((rows, width), BF16),
        pltpu.VMEM((rows, feats), BF16),
        pltpu.VMEM((2, ncol, rows, cw), F32),
        pltpu.VMEM((2, ncol, half, cw), BF16),
        pltpu.VMEM((2, ncol, half, cw), BF16),
        pltpu.VMEM((2, ncol, height, cw), F32),
        pltpu.VMEM((2, ncol, rows, cw), BF16),
        pltpu.VMEM((2, 2, ncol, rows, cw), BF16),
        pltpu.VMEM((2, ncol, rows, cw), BF16),
        pltpu.VMEM((height, feats), F32),
        *final,
        dma((feats // tile_of(feats, 512),)),
        dma((2, tiles)),
        dma((3,)),
        dma((2, 2, tiles)),
        dma((2, bands)),
        dma((2, 2, bands)),
        dma((2, 2, bands)),
        dma((2, 2, bands)),
        dma((2, groups)) if scatter else None,
    ]
    kept = [s is not None for s in scratch]

    def body(*refs):
        fixed, given = refs[:9], iter(refs[9:])
        kernel(shape, *fixed, *[next(given) if k else None for k in kept])

    vmem, anywhere = pl.BlockSpec(memory_space=pltpu.VMEM), pl.BlockSpec(memory_space=pl.ANY)
    out = pl.pallas_call(
        body,
        out_shape=jax.ShapeDtypeStruct((height, block if scatter else width), F32),
        in_specs=[vmem] * 3 + [anywhere] * 5,
        out_specs=vmem,
        scratch_shapes=[s for s in scratch if s is not None],
        compiler_params=pltpu.CompilerParams(
            collective_id=0, has_side_effects=True, vmem_limit_bytes=62 * 1024 * 1024
        ),
        name="attribution",
    )(positions[None], donors[None], encoder_bias, context, targets, beyond_targets, encoder, decoder)
    if not scatter:
        quadrature = lax.psum_scatter(out, ("feat", "path"), scatter_dimension=1, tiled=True)
        ctxb = lax.dynamic_slice_in_dim(context[0], me * block, block, 1)
        offset = ctxb[positions].astype(F32) - ctxb[donors].astype(F32)
        out = offset * quadrature / points
    return out[None]


def solution(mesh):
    shape = tuple(mesh.shape[a] for a in ("layer", "feat", "path"))
    placed = (
        P("layer", None, None),
        P("layer", None, None),
        P(),
        P(),
        P(),
        P("layer", None, "feat"),
        P("layer", "feat"),
        P("layer", None, "feat", "path"),
    )
    return jax.shard_map(
        functools.partial(per_device, shape),
        mesh=mesh,
        in_specs=placed,
        out_specs=P("layer", None, ("feat", "path")),
        check_vma=False,
    )
```

```python
import functools

import jax
import jax.numpy as jnp
from jax import lax
from jax.experimental import pallas as pl
from jax.experimental.pallas import tpu as pltpu
from jax.sharding import PartitionSpec as P

PTS_DEV = 4
LAG = 3
MEET_GRADS = (7, 8, 9)
MESH = pl.DeviceIdType.MESH
NT = (((1,), (1,)), ((), ()))
F32, BF16 = jnp.float32, jnp.bfloat16


def tile_of(width, most):
    sizes = [t for t in range(128, most + 1, 128) if width % t == 0]
    return sizes[-1] if sizes else width


def aligned(start, size):
    return pl.ds(pl.multiple_of(start, size), size)


def chunk_of(cols):
    return 128 if cols % 128 == 0 else cols


def decode_tiles(ncol):
    tiles, at = [], 0
    while at < ncol:
        take = min(2 if at == 0 else 4, ncol - at)
        if ncol - at - take == 1:
            take = min(3, ncol - at)
        if ncol - at == 3:
            take = 3
        tiles.append((at, take))
        at += take
    return tiles


def sent_bands(ncol):
    bands = []
    for i, (start, take) in enumerate(decode_tiles(ncol)):
        at = start
        while at < start + take:
            size = 1 if i == 0 or at + 1 == start + take else 2
            bands.append((at, size, i))
            at += size
    return bands


def kernel(
    shape, pos_ref, don_ref, bias_ref, ctx_hbm, tgt_hbm, bey_hbm, enc_hbm, dec_hbm, out_ref,
    enc, dec, ctx, table, inputs, codes, own, away, away_in, goal, send, recv, err, gsum, part, offsets, final_send, final_recv,
    enc_sem, dec_sem, load_sem, part_sem, in_send, in_recv, err_sem, back_sem, final_sem,
):
    layers, n, paths = shape
    layer, z, path = lax.axis_index("layer"), lax.axis_index("feat"), lax.axis_index("path")
    last = layers - 1
    height, tokens = pos_ref.shape[1], ctx.shape[0]
    rows, width = inputs.shape
    feats, cols = codes.shape[1], dec.shape[2]
    points = rows // height
    half = rows // 2
    cw = chunk_of(cols)
    ncol = cols // cw
    tiles, bands = decode_tiles(ncol), sent_bands(ncol)
    groups = n * paths
    me = z * paths + path
    scatter = final_send is not None

    first = jnp.where(layer == last, 1, lax.rem(layer, 2))
    second = 1 - first
    at_end = (layer == 0) | (layer == last)

    def has_neighbour(k):
        return jnp.where(k == 0, layer > 0, layer < last)

    def neighbour(k):
        return lax.rem(layer + 2 * k - 1 + layers, layers)

    low = n // 2
    upward = z < low
    depth = jnp.where(upward, z, n - 1 - z)
    to_meet = jnp.where(upward, low, n - low) - 1 - depth
    outermost, meets = depth == 0, to_meet == 0
    inner = lax.rem(jnp.where(upward, z + 1, z - 1 + n), n)
    outer = lax.rem(jnp.where(upward, z - 1 + n, z + 1), n)

    barrier = pltpu.get_barrier_semaphore()

    def greet(i, carry):
        pl.semaphore_signal(barrier, inc=1, device_id={"path": lax.rem(path + 1 + i, paths)}, device_id_type=MESH)
        return carry

    lax.fori_loop(0, paths - 1, greet, 0)

    @pl.when(z > 0)
    def _():
        pl.semaphore_signal(barrier, inc=1, device_id={"feat": z - 1}, device_id_type=MESH)

    @pl.when(z < n - 1)
    def _():
        pl.semaphore_signal(barrier, inc=1, device_id={"feat": z + 1}, device_id_type=MESH)

    @pl.when(layer > 0)
    def _():
        pl.semaphore_signal(barrier, inc=1, device_id={"layer": layer - 1}, device_id_type=MESH)

    @pl.when(layer < last)
    def _():
        pl.semaphore_signal(barrier, inc=1, device_id={"layer": layer + 1}, device_id_type=MESH)

    etile = tile_of(feats, 512)
    etiles = feats // etile
    ftile = tile_of(feats, 2048)
    ftiles = feats // ftile

    def enc_copy(j):
        return pltpu.make_async_copy(
            enc_hbm.at[0, :, aligned(j * etile, etile)], enc.at[:, aligned(j * etile, etile)], enc_sem.at[j]
        )

    def columns(at, take):
        return slice(None) if ncol == 1 else pl.ds(pl.multiple_of(at * cw, cw), take * cw)

    def dec_copy(k, i):
        at = columns(*tiles[i])
        return pltpu.make_async_copy(dec_hbm.at[0, k, :, at], dec.at[k, :, at], dec_sem.at[k, i])

    ctx_copy = pltpu.make_async_copy(ctx_hbm.at[0], ctx, load_sem.at[0])
    goal_at = slice(None) if tgt_hbm.shape[2] == cols else aligned(path * cols, cols)
    goal_copies = [
        pltpu.make_async_copy(tgt_hbm.at[0, :, goal_at], table.at[0], load_sem.at[1]),
        pltpu.make_async_copy(bey_hbm.at[:, goal_at], table.at[1], load_sem.at[2]),
    ]

    ctx_copy.start()
    for j in range(etiles):
        enc_copy(j).start()
    for copy in goal_copies:
        copy.start()

    token = lax.broadcasted_iota(jnp.int32, (tokens, height), 0)
    pick_source = (token == pos_ref[...]).astype(F32).T.astype(BF16)
    pick_donor = (token == don_ref[...]).astype(F32).T.astype(BF16)

    def pick(which, rows_of):
        return jnp.dot(which, rows_of, preferred_element_type=F32)

    ctx_copy.wait()
    donor = pick(pick_donor, ctx[...])
    offset = pick(pick_source, ctx[...]) - donor
    for p in range(points):
        inputs[p * height : (p + 1) * height, :] = (donor + ((p + 0.5) / points) * offset).astype(BF16)

    def encode(j, carry):
        enc_copy(j).wait()

        @pl.when(j == max(etiles - 2, 0))
        def _():
            for i in range(len(tiles)):
                for k in (first, second):
                    dec_copy(k, i).start()

        at = aligned(j * etile, etile)
        preact = jnp.dot(inputs[...], enc[:, at], preferred_element_type=F32) + bias_ref[:, at]
        codes[:, at] = jnp.maximum(preact, 0.0).astype(BF16)
        return carry

    lax.fori_loop(0, etiles, encode, 0)

    for copy in goal_copies:
        copy.wait()
    for k in (0, 1):
        value = pick(pick_source, table[k])
        value = jnp.where((z == low - 1) & ((k == 0) | (layer == last)), value, 0.0)
        for m in range(ncol):
            goal[k, m] = value[:, m * cw : (m + 1) * cw]

    around = jnp.minimum(z, 1) + jnp.minimum(n - 1 - z, 1) + jnp.minimum(layer, 1) + jnp.minimum(last - layer, 1)
    pl.semaphore_wait(barrier, paths - 1 + around)

    def half_rows(h):
        return aligned(h * half, half)

    def part_copy(k, i):
        at = pl.ds(*tiles[i])
        return pltpu.make_async_remote_copy(
            away.at[k, at], away_in.at[1 - k, at], part_sem.at[0, k, i], part_sem.at[1, 1 - k, i],
            device_id={"layer": neighbour(k)}, device_id_type=MESH,
        )

    def part_arrival(k, i):
        at = pl.ds(*tiles[i])
        return pltpu.make_async_remote_copy(
            away.at[k, at], away_in.at[k, at], part_sem.at[0, k, i], part_sem.at[1, k, i],
            device_id={"layer": neighbour(k)}, device_id_type=MESH,
        )

    def decode(k, i):
        dec_copy(k, i).wait()
        start, take = tiles[i]
        value = jnp.dot(codes[...], dec[k, :, columns(start, take)], preferred_element_type=F32)
        for c in range(take):
            here = value[:, c * cw : (c + 1) * cw].reshape(points, height, cw) - goal[k, start + c][None]
            own[k, start + c] = here.reshape(rows, cw)

        @pl.when(has_neighbour(k))
        def _():
            for c in range(take):
                away[k, start + c] = own[k, start + c, half_rows(k)].astype(BF16)
            part_copy(k, i).start()

    def place(k, g, whole):
        at, take, _ = bands[g]
        return pl.ds(at, take), slice(None) if whole else half_rows(1 - k)

    def in_copy(k, g, whole):
        at = place(k, g, whole)
        kind = jnp.where(meets, 1, 0)
        return pltpu.make_async_remote_copy(
            send.at[k, *at], recv.at[kind, k, *at], in_send.at[k, g], in_recv.at[kind, k, g],
            device_id={"feat": inner}, device_id_type=MESH,
        )

    def in_arrival(kind, k, g, whole):
        at = place(k, g, whole)
        return pltpu.make_async_remote_copy(
            send.at[k, *at], recv.at[kind, k, *at], in_send.at[k, g], in_recv.at[kind, k, g],
            device_id={"feat": inner}, device_id_type=MESH,
        )

    def err_copy(k, g, whole):
        at = place(k, g, whole)
        return pltpu.make_async_remote_copy(
            err.at[k, *at], err.at[k, *at], err_sem.at[0, k, g], err_sem.at[1, k, g],
            device_id={"feat": outer}, device_id_type=MESH,
        )

    def back_copy(k, g):
        at = place(k, g, False)
        return pltpu.make_async_remote_copy(
            err.at[k, *at], err.at[1 - k, *at], back_sem.at[0, k, g], back_sem.at[1, 1 - k, g],
            device_id={"layer": neighbour(k)}, device_id_type=MESH,
        )

    def back_arrival(k, g):
        at = place(1 - k, g, False)
        return pltpu.make_async_remote_copy(
            err.at[1 - k, *at], err.at[k, *at], back_sem.at[0, k, g], back_sem.at[1, k, g],
            device_id={"layer": neighbour(k)}, device_id_type=MESH,
        )

    def inward(k, g, whole, outermost):
        at = place(k, g, whole)
        base = own[k, *at]
        if not whole:
            tile = bands[g][2]
            if bands[g][0] == tiles[tile][0]:
                part_arrival(k, tile).wait_recv()
            base = base + away_in[k, at[0]].astype(F32)
        if not outermost:
            in_arrival(0, k, g, whole).wait_recv()
            base = base + recv[0, k, *at].astype(F32)
        send[k, *at] = base.astype(BF16)
        in_copy(k, g, whole).start()

    def finish(k, g, whole, meets, outermost):
        at = place(k, g, whole)
        if meets:
            in_arrival(1, k, g, whole).wait_recv()
            err[k, *at] = (send[k, *at].astype(F32) + recv[1, k, *at].astype(F32)).astype(BF16)
        else:
            err_copy(k, g, whole).wait_recv()
        if not outermost:
            err_copy(k, g, whole).start()
        if not whole:
            back_copy(k, g).start()

    def grads_step(k, gs):
        units = [u for g in gs for u in range(bands[g][0], bands[g][0] + bands[g][1])]
        here = columns(units[0], len(units))

        def of_tile(j, carry):
            f_at = aligned(j * ftile, ftile)
            errors = jnp.concatenate([err[k, u] for u in units], axis=1)
            grads = lax.dot_general(errors, dec[k, f_at, here], NT, preferred_element_type=F32)
            gated = jnp.where(codes[:, f_at].astype(F32) > 0, grads, 0.0)
            gsum[:, f_at] += gated.reshape(points, height, ftile).sum(axis=0)
            return carry

        lax.fori_loop(0, ftiles, of_tile, 0)

    gsum[...] = jnp.zeros_like(gsum)

    count = len(tiles)
    of_tile = [[g for g in range(len(bands)) if bands[g][2] == i] for i in range(count)] + [[]]
    order, step_of = [], []
    for i in range(count + 1):
        order += [(0, g) for g in of_tile[i]] + [(1, g) for g in (of_tile[i - 1] if i else [])]
        step_of += [i] * (len(order) - len(step_of))
    together = [of_tile[0]] + [[g] for i in range(1, count) for g in of_tile[i]]
    all_grads = [(s, gs) for gs in together for s in (0, 1)]

    def band(act, s, g, is_end=None):
        if s:
            act(second, g, False)
        elif is_end is None:
            pl.when(at_end)(lambda: act(first, g, True))
            pl.when(~at_end)(lambda: act(first, g, False))
        else:
            act(first, g, is_end)

    def run_grads(s, gs):
        def arrive(k):
            for g in gs:
                back_arrival(k, g).wait_recv()

        if s:
            arrive(second)
        else:
            pl.when(~at_end)(lambda: arrive(first))
        grads_step(second if s else first, gs)

    def role(meets, outermost, stage=None):
        push = functools.partial(inward, outermost=outermost)
        pull = functools.partial(finish, meets=meets, outermost=outermost)
        ahead = min(LAG, len(order)) if meets else len(order)

        if stage is not None:
            i, s = stage
            limit = i - 1 if meets else i
            if s == (1 if meets else 0):
                for item, step in zip(order[:ahead], step_of):
                    if step == limit:
                        band(push, *item, True)
            return

        def start(is_end):
            for item, step in zip(order[:ahead], step_of):
                if not is_end or step > count - (2 if meets else 1):
                    band(push, *item, is_end)

        pl.when(at_end)(lambda: start(True))
        pl.when(~at_end)(lambda: start(False))
        left = list(all_grads)
        for j, item in enumerate(order):
            if j + ahead < len(order):
                band(push, *order[j + ahead])
            band(pull, *item)
            if not meets or j in MEET_GRADS:
                ready = [x for x in left if all((x[0], g) in order[: max(j - 1, 0)] for g in x[1])]
                for x in ready[: 1 if meets else None]:
                    run_grads(*x)
                    left.remove(x)
        for x in left:
            run_grads(*x)

    def roles(stage, allowed):
        if low == 1:
            pl.when(allowed)(lambda: role(True, True, stage))
        else:
            pl.when(meets & allowed)(lambda: role(True, False, stage))
            pl.when(outermost & allowed)(lambda: role(False, True, stage))
            if n > 4:
                pl.when(~meets & ~outermost & allowed)(lambda: role(False, False, stage))

    for i in range(count):
        for s in (0, 1):
            decode(second if s else first, i)
            roles((i, s), at_end)
    roles(None, layer >= 0)

    if scatter:
        block = width // groups
        gated_sum = gsum[...].astype(BF16)

        def final_copy(sender, target):
            return pltpu.make_async_remote_copy(
                final_send.at[target], final_recv.at[sender], final_sem.at[0, target], final_sem.at[1, sender],
                device_id={"feat": target // paths, "path": lax.rem(target, paths)}, device_id_type=MESH,
            )

        side = groups // 2

        def send_side(i, carry):
            which = jnp.where(2 * z < n, 1 - i, i)
            at = aligned(which * side * block, side * block)
            product = lax.dot_general(gated_sum, enc[at, :], NT, preferred_element_type=F32)
            for c in range(side):
                b = which * side + c
                value = product[:, c * block : (c + 1) * block]

                @pl.when(b == me)
                def _():
                    part[...] = value

                @pl.when(b != me)
                def _():
                    final_send[b] = value.astype(BF16)
                    final_copy(me, b).start()

            return carry

        lax.fori_loop(0, 2, send_side, 0)
        for b in range(groups):
            offsets[b] = offset[:, b * block : (b + 1) * block]

        def take_block(i, carry):
            b = lax.rem(me + 1 + i, groups)
            final_copy(b, b).wait_recv()
            part[...] += final_recv[b].astype(F32)
            return carry

        lax.fori_loop(0, groups - 1, take_block, 0)
        out_ref[...] = offsets[me] * part[...] / points

        def sent_block(i, carry):
            b = lax.rem(me + 1 + i, groups)
            final_copy(me, b).wait_send()
            return carry

        lax.fori_loop(0, groups - 1, sent_block, 0)
    else:
        out_ref[...] = lax.dot_general(gsum[...].astype(BF16), enc[...], NT, preferred_element_type=F32)

    for i in range(len(tiles)):
        for k in (0, 1):

            @pl.when(has_neighbour(k))
            def _():
                part_copy(k, i).wait_send()

    def sent(k, g, whole):
        in_copy(k, g, whole).wait_send()

        @pl.when(~outermost)
        def _():
            err_copy(k, g, whole).wait_send()

        if not whole:
            back_copy(k, g).wait_send()

    for s, g in order:
        band(sent, s, g)


def per_device(shape, context, targets, beyond_targets, positions, donors, encoder, encoder_bias, decoder):
    layers, n, paths = shape
    path = lax.axis_index("path")
    height = positions.shape[0]
    tokens = context.shape[1]
    width, feats = encoder.shape[1:]
    cols = decoder.shape[3]
    points = PTS_DEV * paths
    rows = points * height
    half = rows // 2
    groups = n * paths
    block = width // groups
    me = lax.axis_index("feat") * paths + path
    scatter = block % 16 == 0 and groups % 2 == 0
    if cols % 128:
        targets = lax.dynamic_slice_in_dim(targets, path * cols, cols, 2)
        beyond_targets = lax.dynamic_slice_in_dim(beyond_targets, path * cols, cols, 1)
    dma = pltpu.SemaphoreType.DMA
    cw = chunk_of(cols)
    ncol = cols // cw
    tiles, bands = len(decode_tiles(ncol)), len(sent_bands(ncol))
    final = (
        [
            pltpu.VMEM((height, block), F32),
            pltpu.VMEM((groups, height, block), F32),
            pltpu.VMEM((groups, height, block), BF16),
            pltpu.VMEM((groups, height, block), BF16),
        ]
        if scatter
        else [None, None, None, None]
    )
    scratch = [
        pltpu.VMEM((width, feats), BF16),
        pltpu.VMEM((2, feats, cols), BF16),
        pltpu.VMEM((tokens, width), BF16),
        pltpu.VMEM((2, tokens, cols), BF16),
        pltpu.VMEM((rows, width), BF16),
        pltpu.VMEM((rows, feats), BF16),
        pltpu.VMEM((2, ncol, rows, cw), F32),
        pltpu.VMEM((2, ncol, half, cw), BF16),
        pltpu.VMEM((2, ncol, half, cw), BF16),
        pltpu.VMEM((2, ncol, height, cw), F32),
        pltpu.VMEM((2, ncol, rows, cw), BF16),
        pltpu.VMEM((2, 2, ncol, rows, cw), BF16),
        pltpu.VMEM((2, ncol, rows, cw), BF16),
        pltpu.VMEM((height, feats), F32),
        *final,
        dma((feats // tile_of(feats, 512),)),
        dma((2, tiles)),
        dma((3,)),
        dma((2, 2, tiles)),
        dma((2, bands)),
        dma((2, 2, bands)),
        dma((2, 2, bands)),
        dma((2, 2, bands)),
        dma((2, groups)) if scatter else None,
    ]
    kept = [s is not None for s in scratch]

    def body(*refs):
        fixed, given = refs[:9], iter(refs[9:])
        kernel(shape, *fixed, *[next(given) if k else None for k in kept])

    vmem, anywhere = pl.BlockSpec(memory_space=pltpu.VMEM), pl.BlockSpec(memory_space=pl.ANY)
    out = pl.pallas_call(
        body,
        out_shape=jax.ShapeDtypeStruct((height, block if scatter else width), F32),
        in_specs=[vmem] * 3 + [anywhere] * 5,
        out_specs=vmem,
        scratch_shapes=[s for s in scratch if s is not None],
        compiler_params=pltpu.CompilerParams(
            collective_id=0, has_side_effects=True, vmem_limit_bytes=62 * 1024 * 1024
        ),
        name="attribution",
    )(positions[None], donors[None], encoder_bias, context, targets, beyond_targets, encoder, decoder)
    if not scatter:
        quadrature = lax.psum_scatter(out, ("feat", "path"), scatter_dimension=1, tiled=True)
        ctxb = lax.dynamic_slice_in_dim(context[0], me * block, block, 1)
        offset = ctxb[positions].astype(F32) - ctxb[donors].astype(F32)
        out = offset * quadrature / points
    return out[None]


def solution(mesh):
    shape = tuple(mesh.shape[a] for a in ("layer", "feat", "path"))
    placed = (
        P("layer", None, None),
        P("layer", None, None),
        P(),
        P(),
        P(),
        P("layer", None, "feat"),
        P("layer", "feat"),
        P("layer", None, "feat", "path"),
    )
    return jax.shard_map(
        functools.partial(per_device, shape),
        mesh=mesh,
        in_specs=placed,
        out_specs=P("layer", None, ("feat", "path")),
        check_vma=False,
    )
```
